256 devices in a mesh: tok: 32 (over x, y, core), tp: 8 (over z).
Axes of the slice: x: 4, y: 4, z: 8, core: 2. Of those that a mesh axis runs over, the one named last changes fastest.
Arguments:
- hidden: bfloat16 [2048, 7168], P('tok'), may hold values from -6 to 6
- ln_gain: float32 [7168], replicated, may hold values from 0.1 to 1.9
- ln_bias: float32 [7168], replicated, may hold values from -3 to 3
- w_qkv: bfloat16 [7168, 3, 7168], P('tok', None, 'tp'), may hold values from -0.0625 to 0.0625
- qkv_bias: float32 [3, 7168], P(None, 'tp'), may hold values from -3 to 3
- w_out: bfloat16 [7168, 7168], P('tp', 'tok'), may hold values from -0.0625 to 0.0625
- out_bias: float32 [7168], replicated, may hold values from -3 to 3
- dec_cache: bfloat16 [64, 1024, 2, 7168], P('tok', None, None, 'tp'), may hold values from -8 to 8
- prior_kv: bfloat16 [512, 2, 2, 7168], P('tok', None, None, 'tp'), may hold values from -8 to 8
- dec_len: int32 [64], P('tok'), may hold values from 1 to 1024, as said below
- offsets: int32 [2], replicated, may hold values from 4 to 512, as said below
Outputs:
- result: bfloat16 [2048, 7168], P('tok')
- new_kv: bfloat16 [2048, 2, 7168], P('tok', None, 'tp')
The draws below stay inside these ranges and needn't reach their ends.
Inputs may be any that keep to these rules, and one draw needn't show every extreme that they name: `dec_len`: each decode request has 1 to 1024 cached positions; some request has exactly 1024. `offsets`: each prefill block follows 4 to 512 earlier positions; one of the two follows exactly 512.
All inputs are finite; a program needn't handle non-finite values.
Results may differ from the reference program's by a relative error of at most 0.015.
Values may be sent and summed in bfloat16 or wider, within the bound.
No kernel may reach another device: no remote copies, remote signals or barrier semaphores. Data moves between devices by JAX's collectives and lax.ppermute only.
A program may use at most 128 MiB of HBM per device.

```python
import jax
import jax.numpy as jnp
from jax import lax

D = 7168
HEADS = 56
HEAD = 128
PRE_DEV = 62
DEC_DEV = 2
LMAX = 1024
WINDOW = 512
SINKS = 4
TOK_DEV = 64
TOKENS = 2048
SPAN = 992
REQS = 64
PCTX = 512
HD = 7168
N_TOK = 32


def draw_dec_len(key, part):
    lengths = jax.random.randint(jax.random.fold_in(key, 11), (REQS,), 1, LMAX + 1)
    chosen = jax.random.randint(jax.random.fold_in(key, 12), (), 0, REQS)
    return jnp.where(jnp.arange(REQS) == chosen, LMAX, lengths).astype(jnp.int32)


def draw_offsets(key, part):
    starts = jax.random.randint(jax.random.fold_in(key, 21), (2,), SINKS, PCTX + 1)
    chosen = jax.random.randint(jax.random.fold_in(key, 22), (), 0, 2)
    return jnp.where(jnp.arange(2) == chosen, PCTX, starts).astype(jnp.int32)


def draw_qkv_bias(key, part):
    base = 0.5 * jax.random.truncated_normal(jax.random.fold_in(key, 51), -6.0, 6.0, (3, HD), jnp.float32)
    return base.astype(jnp.float32)


def draw_dec_cache(key, part):
    base = jax.random.truncated_normal(jax.random.fold_in(key, 61), -6.0, 6.0, (REQS, LMAX, 2, HD), jnp.float32)
    return base.astype(jnp.bfloat16)


def draw_prior_kv(key, part):
    base = jax.random.truncated_normal(jax.random.fold_in(key, 71), -6.0, 6.0, (PCTX, 2, 2, HD), jnp.float32)
    return base.astype(jnp.bfloat16)


def steps_of(stream_key, shape, cuts, low, high):
    level = 1.0
    for dim, parts in cuts:
        heights = jax.random.uniform(jax.random.fold_in(jax.random.fold_in(stream_key, 6), dim), (parts,), jnp.float32, low / len(cuts), high / len(cuts))
        level = level * jnp.repeat(jnp.exp(heights), shape[dim] // parts).reshape((-1,) + (1,) * (len(shape) - 1 - dim))
    return level


def bell_draw(own_key, shape, scale, reach, cuts=(), kind=jnp.bfloat16):
    drawn = jax.random.normal(own_key, shape, jnp.float32) * scale
    if len(cuts) > 0:
        drawn = steps_of(own_key, shape, cuts, -0.22, 0.18) * drawn
    return jnp.clip(drawn, min=-reach, max=reach).astype(kind)


def setup_inputs(seed: int = 0) -> dict:
    key_list = jax.random.split(jax.random.key(seed), 12)
    return {
        "hidden": bell_draw(key_list[0], (TOKENS, D), 1.0, 6.0, ((0, 32),)),
        "ln_gain": jnp.clip(1.0 + 0.18 * jax.random.normal(key_list[1], (D,), jnp.float32), 0.1, 1.9),
        "ln_bias": bell_draw(key_list[2], (D,), 0.5, 3.0, (), jnp.float32),
        "w_qkv": bell_draw(key_list[3], (D, 3, HD), D ** -0.5, 0.0625, ((0, 32), (2, 8))),
        "qkv_bias": draw_qkv_bias(jax.random.fold_in(key_list[11], 71), 0),
        "w_out": bell_draw(key_list[5], (HD, D), HD ** -0.5, 0.0625, ((0, 8), (1, 32))),
        "out_bias": bell_draw(key_list[6], (D,), 0.5, 3.0, (), jnp.float32),
        "dec_cache": draw_dec_cache(jax.random.fold_in(key_list[11], 71), 0),
        "prior_kv": draw_prior_kv(jax.random.fold_in(key_list[11], 71), 0),
        "dec_len": draw_dec_len(jax.random.fold_in(key_list[11], 71), 0),
        "offsets": draw_offsets(jax.random.fold_in(key_list[11], 71), 0),
    }


NEG = -1e+30

def masked_attention(queries, keys, values, allowed):
    scores = jnp.dot(queries, keys.T, preferred_element_type=jnp.float32)
    scores = jnp.where(allowed, scores, NEG)
    highest = lax.optimization_barrier(jnp.max(scores, axis=1, keepdims=True))
    expd = jnp.where(allowed, jnp.exp(scores - highest), 0.0)
    weighted = jnp.dot(expd.astype(jnp.bfloat16), values, preferred_element_type=jnp.float32)
    return weighted / lax.optimization_barrier(jnp.sum(expd, axis=1, keepdims=True))

def reference(hidden, ln_gain, ln_bias, w_qkv, qkv_bias, w_out, out_bias, dec_cache, prior_kv, dec_len, offsets):
    inputs = hidden.astype(jnp.float32)
    average = lax.optimization_barrier(jnp.mean(inputs, axis=1, keepdims=True))
    spread = lax.optimization_barrier(jnp.mean((inputs - average) ** 2, axis=1, keepdims=True))
    normed = ((inputs - average) / jnp.sqrt(spread + 1e-05) * ln_gain + ln_bias).astype(jnp.bfloat16)
    projected = jnp.dot(normed, w_qkv.reshape(D, 3 * HD), preferred_element_type=jnp.float32).reshape(TOKENS, 3, HD) + qkv_bias[None]
    factors = jnp.array([HEAD ** (-0.5), 1.0, 1.0], jnp.float32)
    qkv = (projected * factors[None, :, None]).astype(jnp.bfloat16)
    new_kv = qkv[:, 1:]
    grid = qkv.reshape(N_TOK, TOK_DEV, 3, HD)
    prefill = grid[:, :PRE_DEV].reshape(N_TOK * PRE_DEV, 3, HD)
    decode = grid[:, PRE_DEV:].reshape(REQS, 3, HD)
    pieces = []
    for block in range(2):
        start = offsets[block]
        block_rows = prefill[block * SPAN:(block + 1) * SPAN]
        keys = jnp.concatenate([prior_kv[:, block, 0], block_rows[:, 1]], axis=0)
        values = jnp.concatenate([prior_kv[:, block, 1], block_rows[:, 2]], axis=0)
        earlier = jnp.arange(PCTX, dtype=jnp.int32)
        query_pos = start + jnp.arange(SPAN, dtype=jnp.int32)
        key_pos = jnp.concatenate([earlier, query_pos])
        key_valid = jnp.concatenate([earlier < start, jnp.ones((SPAN,), bool)])
        allowed = key_valid[None] & (key_pos[None] <= query_pos[:, None]) & ((key_pos[None] < SINKS) | (key_pos[None] > query_pos[:, None] - WINDOW))
        q_heads = block_rows[:, 0].reshape(SPAN, HEADS, HEAD).transpose(1, 0, 2)
        k_heads = keys.reshape(-1, HEADS, HEAD).transpose(1, 0, 2)
        v_heads = values.reshape(-1, HEADS, HEAD).transpose(1, 0, 2)
        output = lax.map(lambda triple: masked_attention(triple[0], triple[1], triple[2], allowed), (q_heads, k_heads, v_heads))
        pieces.append(output.transpose(1, 0, 2).reshape(SPAN, HD))
    prefill_out = jnp.concatenate(pieces, axis=0)

    def one_request(triple):
        row, cache, length = triple
        query = row[0].reshape(HEADS, HEAD).astype(jnp.float32)
        keys = jnp.concatenate([cache[:, 0], row[1][None]], axis=0).reshape(LMAX + 1, HEADS, HEAD).astype(jnp.float32)
        values = jnp.concatenate([cache[:, 1], row[2][None]], axis=0).reshape(LMAX + 1, HEADS, HEAD)
        key_pos = jnp.arange(LMAX + 1, dtype=jnp.int32)
        allowed = (key_pos < length) & ((key_pos < SINKS) | (key_pos > length - WINDOW)) | (key_pos == LMAX)
        scores = jnp.einsum('hd,khd->hk', query, keys, precision=lax.Precision.HIGHEST)
        scores = jnp.where(allowed[None], scores, NEG)
        highest = lax.optimization_barrier(jnp.max(scores, axis=1, keepdims=True))
        expd = jnp.where(allowed[None], jnp.exp(scores - highest), 0.0)
        weighted = jnp.einsum('hk,khd->hd', expd.astype(jnp.bfloat16).astype(jnp.float32), values.astype(jnp.float32), precision=lax.Precision.HIGHEST)
        return weighted / lax.optimization_barrier(jnp.sum(expd, axis=1, keepdims=True))
    decode_out = lax.map(one_request, (decode, dec_cache, dec_len)).reshape(REQS, HD)
    attn = jnp.concatenate([prefill_out.reshape(N_TOK, PRE_DEV, HD), decode_out.reshape(N_TOK, DEC_DEV, HD)], axis=1)
    attn = attn.reshape(TOKENS, HD).astype(jnp.bfloat16)
    result = (inputs + jnp.dot(attn, w_out, preferred_element_type=jnp.float32) + out_bias).astype(jnp.bfloat16)
    return (result, new_kv)
```

```python
import jax
import jax.numpy as jnp
from jax import lax
from jax.experimental import pallas as pl
from jax.experimental.pallas import tpu as pltpu
from jax.sharding import Mesh, PartitionSpec as P

HEAD = 128
WINDOW = 512
SINKS = 4
NEG = -1e30
XS, YS, CS, ZS = 4, 4, 2, 8
GROUP = YS * CS


def shift(axis_size, step):
    return [(i, (i + step) % axis_size) for i in range(axis_size)]


def norm_kernel(hid_ref, gain_ref, bias_ref, out_ref):
    rows, width = hid_ref.shape
    inputs = hid_ref[...].astype(jnp.float32)
    average = jnp.mean(inputs, axis=1, keepdims=True)
    centered = inputs - average
    spread = jnp.mean(centered * centered, axis=1, keepdims=True)
    normed = centered / jnp.sqrt(spread + 1e-05) * gain_ref[...] + bias_ref[...]
    piece = out_ref.shape[3]
    for block in range(XS):
        for member in range(GROUP):
            first = (block * GROUP + member) * piece
            out_ref[member, block] = normed[:, first : first + piece].astype(jnp.bfloat16)


def normalise(hidden, gain, bias):
    rows, width = hidden.shape
    piece = width // (XS * GROUP)
    return pl.pallas_call(
        norm_kernel,
        out_shape=jax.ShapeDtypeStruct((GROUP, XS, rows, piece), jnp.bfloat16),
        name="norm",
    )(hidden, gain[None], bias[None])


def qkv_kernel(where_ref, in_ref, own_ref, left_ref, right_ref, far_a_ref, far_b_ref, out_ref):
    me = where_ref[0]
    members, _, rows, piece = in_ref.shape

    def rows_of(step):
        block = lax.rem(me + step, XS)
        return in_ref[:, pl.ds(block, 1)].reshape(members * rows, piece)

    def wide(ref):
        return jnp.concatenate([ref[0], ref[1], ref[2]], axis=1)

    def product(left, right):
        return jnp.dot(left, right, preferred_element_type=jnp.float32)

    far = jnp.concatenate([wide(far_a_ref), wide(far_b_ref)], axis=0)
    total = product(rows_of(0), wide(own_ref)) + product(rows_of(3), wide(left_ref))
    total += product(rows_of(1), wide(right_ref)) + product(rows_of(2), far)
    out_ref[0] = total.astype(jnp.bfloat16)


def project(where, pieces, own, left, right, far_a, far_b):
    members, blocks, rows, piece = pieces.shape
    heads = own.shape[2] // HEAD

    def head_map(step, where_ref):
        return (0, 0, jnp.minimum(CS * step + where_ref[1], heads - 1))

    def weight_spec(array):
        return pl.BlockSpec((3, array.shape[1], HEAD), head_map)

    return pl.pallas_call(
        qkv_kernel,
        out_shape=jax.ShapeDtypeStruct((YS, members * rows, 3 * HEAD), jnp.bfloat16),
        grid_spec=pltpu.PrefetchScalarGridSpec(
            num_scalar_prefetch=1,
            grid=(YS,),
            in_specs=[pl.BlockSpec(pieces.shape, lambda step, w: (0, 0, 0, 0))]
            + [weight_spec(a) for a in (own, left, right, far_a, far_b)],
            out_specs=pl.BlockSpec((1, members * rows, 3 * HEAD), lambda step, w: (step, 0, 0)),
        ),
        name="project",
    )(where, pieces, own, left, right, far_a, far_b)


def attend_kernel(pre_dev, where_ref, query_ref, key_ref, value_ref, last_key_ref, last_value_ref, prior_ref, out_ref):
    odd = where_ref[0]
    start = where_ref[1]
    queries = query_ref[...]
    count = queries.shape[0]
    rows = key_ref.shape[0]
    tok_rows = rows // GROUP
    half = pre_dev * GROUP

    def local(index):
        return (index // tok_rows) * pre_dev + index % tok_rows

    row = pl.program_id(0) * count + lax.broadcasted_iota(jnp.int32, (count, 1), 0)
    query_pos = start + odd * half + local(row)
    key_row = lax.broadcasted_iota(jnp.int32, (1, rows), 1)
    is_prefill = key_row % tok_rows < pre_dev
    own_pos = start + odd * half + local(key_row)
    last_pos = start + local(key_row)
    old = prior_ref.shape[0] * prior_ref.shape[2]
    old_pos = lax.broadcasted_iota(jnp.int32, (1, old), 1)
    key_pos = jnp.concatenate([own_pos, last_pos, old_pos], axis=1)
    key_valid = jnp.concatenate(
        [
            is_prefill.astype(jnp.int32),
            is_prefill.astype(jnp.int32) * odd,
            (old_pos < start).astype(jnp.int32),
        ],
        axis=1,
    )
    prior_keys = prior_ref[:, 0].reshape(old, HEAD)
    prior_values = prior_ref[:, 1].reshape(old, HEAD)

    def score(keys):
        return lax.dot_general(
            queries, keys, (((1,), (1,)), ((), ())), preferred_element_type=jnp.float32
        )

    scores = jnp.concatenate(
        [score(key_ref[...]), score(last_key_ref[...]), score(prior_keys)], axis=1
    )
    key_pos = jnp.where(key_valid > 0, key_pos, 1 << 20)
    allowed = (key_pos <= query_pos) & ((key_pos < SINKS) | (key_pos > query_pos - WINDOW))
    scores = jnp.where(allowed, scores, NEG)
    highest = jnp.max(scores, axis=1, keepdims=True)
    expd = jnp.exp(scores - highest)
    totals = jnp.sum(expd, axis=1, keepdims=True)
    weights = expd.astype(jnp.bfloat16)

    def weigh(part, values):
        return jnp.dot(part, values, preferred_element_type=jnp.float32)

    weighted = (
        weigh(weights[:, :rows], value_ref[...])
        + weigh(weights[:, rows : 2 * rows], last_value_ref[...])
        + weigh(weights[:, 2 * rows :], prior_values)
    )
    out_ref[...] = (weighted / totals).astype(jnp.bfloat16)


def attend(pre_dev, where, qkv, last, prior):
    rows = qkv.shape[0]
    step_rows = 128

    def column(width, index):
        return pl.BlockSpec((rows, HEAD), lambda i, w, index=index: (0, index))

    import functools

    return pl.pallas_call(
        functools.partial(attend_kernel, pre_dev),
        out_shape=jax.ShapeDtypeStruct((rows, HEAD), jnp.bfloat16),
        grid_spec=pltpu.PrefetchScalarGridSpec(
            num_scalar_prefetch=1,
            grid=(rows // step_rows,),
            in_specs=[
                pl.BlockSpec((step_rows, HEAD), lambda i, w: (i, 0)),
                column(3, 1),
                column(3, 2),
                column(2, 0),
                column(2, 1),
                pl.BlockSpec(prior.shape, lambda i, w: (0, 0, 0, 0)),
            ],
            out_specs=pl.BlockSpec((step_rows, HEAD), lambda i, w: (i, 0)),
        ),
        name="attend",
    )(where, qkv, qkv, qkv, last, last, prior)


def decode(queries, own_keys, own_values, cache, lengths):
    requests, slots = cache.shape[0], cache.shape[1]
    heads = queries.shape[1]
    outs = []
    for request in range(requests):
        keys = cache[request, :, 0].reshape(slots, heads, HEAD)
        values = cache[request, :, 1].reshape(slots, heads, HEAD)
        length = lengths[request]
        slot = jnp.arange(slots, dtype=jnp.int32)
        allowed = (slot < length) & ((slot < SINKS) | (slot > length - WINDOW))
        query = queries[request]
        scores = jnp.einsum(
            "qhd,khd->hqk", query[None], keys, preferred_element_type=jnp.float32
        )[:, 0]
        own = jnp.sum(query.astype(jnp.float32) * own_keys[request].astype(jnp.float32), axis=1)
        scores = jnp.where(allowed[None], scores, NEG)
        highest = jnp.maximum(jnp.max(scores, axis=1), own)
        expd = jnp.where(allowed[None], jnp.exp(scores - highest[:, None]), 0.0)
        own_expd = jnp.exp(own - highest)
        totals = jnp.sum(expd, axis=1) + own_expd
        weighted = jnp.einsum(
            "hqk,khd->qhd",
            expd.astype(jnp.bfloat16)[:, None],
            values,
            preferred_element_type=jnp.float32,
        )[0]
        own_weight = own_expd.astype(jnp.bfloat16).astype(jnp.float32)
        weighted = weighted + own_weight[:, None] * own_values[request].astype(jnp.float32)
        outs.append(weighted / totals[:, None])
    return jnp.stack(outs, axis=0).astype(jnp.bfloat16)


def on_device(
    hidden,
    ln_gain,
    ln_bias,
    w_qkv,
    qkv_bias,
    w_out,
    out_bias,
    dec_cache,
    prior_kv,
    dec_len,
    offsets,
):
    me_x = lax.axis_index("x")
    me_c = lax.axis_index("c")
    me_z = lax.axis_index("z")
    member = lax.axis_index("y") * CS + me_c
    tok_rows, width = hidden.shape
    dec_dev, lmax = dec_cache.shape[0], dec_cache.shape[1]
    pre_dev = tok_rows - dec_dev
    head_width = w_qkv.shape[2]
    heads = head_width // HEAD
    pcb = prior_kv.shape[0]
    rows = GROUP * tok_rows
    block = me_x // 2
    start = jnp.where(block == 0, offsets[0], offsets[1])

    own = w_qkv.transpose(1, 0, 2)
    half = own.shape[1] // 2
    left = lax.ppermute(own, "x", shift(XS, 1))
    right = lax.ppermute(own, "x", shift(XS, -1))
    far_a = lax.ppermute(left[:, :half], "x", shift(XS, 1))
    far_b = lax.ppermute(right[:, half:], "x", shift(XS, -1))

    prior = prior_kv.reshape(pcb, 2, 2, heads, HEAD)
    prior = jnp.pad(prior, ((0, 0), (0, 0), (0, 0), (0, GROUP - heads), (0, 0)))
    prior = prior.transpose(1, 3, 2, 0, 4)
    prior = jnp.repeat(prior, 2, axis=0).reshape(XS * GROUP, 2, pcb, HEAD)
    prior = lax.all_to_all(prior, ("x", "y", "c"), 0, 0, tiled=True)

    pieces = normalise(hidden, ln_gain, ln_bias)
    pieces = lax.all_to_all(pieces, ("y", "c"), 0, 0, tiled=True)

    send = project(jnp.stack([me_x, 1 - me_c]), pieces, own, left, right, far_a, far_b)
    swapped = lax.ppermute(send, "c", [(0, 1), (1, 0)])
    keep = project(jnp.stack([me_x, me_c]), pieces, own, left, right, far_a, far_b)
    partial = (keep.astype(jnp.float32) + swapped.astype(jnp.float32)).astype(jnp.bfloat16)
    partial = lax.all_to_all(partial, "y", 0, 0, tiled=True)

    my_head = jnp.minimum(member, heads - 1)
    bias = lax.dynamic_slice(qkv_bias, (0, my_head * HEAD), (3, HEAD)).reshape(1, 3 * HEAD)
    lane = lax.broadcasted_iota(jnp.int32, (1, 3 * HEAD), 1)
    factors = jnp.where(lane < HEAD, HEAD ** (-0.5), 1.0)
    qkv = ((jnp.sum(partial.astype(jnp.float32), axis=0) + bias) * factors).astype(jnp.bfloat16)

    last = lax.ppermute(qkv[:, HEAD:], "x", [(0, 1), (2, 3)])
    mine = lax.all_to_all(qkv.reshape(GROUP, tok_rows, 3 * HEAD), ("y", "c"), 0, 0, tiled=True)
    mine = mine[:heads].reshape(heads, tok_rows, 3, HEAD)
    new_kv = mine[:, :, 1:].transpose(1, 2, 0, 3).reshape(tok_rows, 2, head_width)
    dec_rows = mine[:, pre_dev:].transpose(1, 2, 0, 3)
    decoded = decode(dec_rows[:, 0], dec_rows[:, 1], dec_rows[:, 2], dec_cache, dec_len)

    prefilled = attend(pre_dev, jnp.stack([me_x % 2, start]), qkv, last, prior)

    tied, w_tied = lax.optimization_barrier((partial, w_out))
    w_turned = w_tied.T
    others = [lax.ppermute(w_turned, "x", shift(XS, step)) for step in (1, -1, 2)]

    flat = decoded.reshape(dec_dev * heads, HEAD)
    extra = 16
    flat = jnp.pad(flat, ((0, extra - dec_dev * heads), (0, 0)))
    payload = jnp.concatenate([prefilled, flat], axis=0)
    payload = jnp.broadcast_to(payload[None], (GROUP, rows + extra, HEAD))
    gathered = lax.all_to_all(payload, ("y", "c"), 0, 0, tiled=True)
    from_prefill = gathered[:heads, :rows].reshape(heads, GROUP, tok_rows, HEAD)[:, :, :pre_dev]
    from_decode = gathered[:, rows : rows + dec_dev * heads].reshape(GROUP, dec_dev, heads, HEAD)
    attn = jnp.concatenate([from_prefill, from_decode.transpose(2, 0, 1, 3)], axis=2)
    attn = attn.transpose(1, 2, 0, 3).reshape(rows, head_width)

    stacked = jnp.stack([w_turned] + others, axis=0)
    order = lax.rem(jnp.array([0, 3, 1, 2], jnp.int32)[None], XS)
    del order
    piece = stacked.shape[1]
    cols = lax.dot_general(
        attn,
        stacked.reshape(XS * piece, head_width),
        (((1,), (1,)), ((), ())),
        preferred_element_type=jnp.float32,
    ).astype(jnp.bfloat16)
    shares = cols.reshape(GROUP * ZS, tok_rows // ZS, XS * piece)
    shares = lax.all_to_all(shares, ("y", "c", "z"), 0, 0, tiled=True)
    shares = shares.reshape(GROUP, ZS, tok_rows // ZS, XS, piece)
    summed = jnp.sum(shares.astype(jnp.float32), axis=1)
    parts = [summed[:, :, i] for i in range(XS)]
    choose = [[0, 2, 3, 1], [1, 0, 2, 3], [3, 1, 0, 2], [2, 3, 1, 0]]
    ordered = []
    for target in range(XS):
        value = parts[choose[0][target]]
        for here in range(1, XS):
            value = jnp.where(me_x == here, parts[choose[here][target]], value)
        ordered.append(value)
    total = jnp.stack(ordered, axis=0).transpose(2, 0, 1, 3).reshape(tok_rows // ZS, width)
    slab = tok_rows // ZS
    residual = lax.dynamic_slice(hidden, (me_z * slab, 0), (slab, width)).astype(jnp.float32)
    result = (residual + total + out_bias).astype(jnp.bfloat16)
    result = jnp.broadcast_to(result[None], (ZS, slab, width))
    result = lax.all_to_all(result, "z", 0, 0, tiled=True).reshape(tok_rows, width)
    return (result, new_kv)


def solution(mesh):
    fine = Mesh(mesh.devices.reshape(XS, YS, CS, ZS), ("x", "y", "c", "z"))
    tok = ("x", "y", "c")
    in_specs = (
        P(tok, None),
        P(),
        P(),
        P(tok, None, "z"),
        P(None, "z"),
        P("z", tok),
        P(),
        P(tok, None, None, "z"),
        P(tok, None, None, "z"),
        P(tok),
        P(),
    )
    out_specs = (P(tok, None), P(tok, None, "z"))
    return jax.shard_map(
        on_device, mesh=fine, in_specs=in_specs, out_specs=out_specs, check_vma=False
    )
```

```python
import functools

import jax
import jax.numpy as jnp
from jax import lax
from jax.experimental import pallas as pl
from jax.experimental.pallas import tpu as pltpu
from jax.sharding import Mesh, PartitionSpec as P

HEAD = 128
WINDOW = 512
SINKS = 4
NEG = -1e30
FAR_AWAY = 1 << 20
XS, YS, CS, ZS = 4, 4, 2, 8
GROUP = YS * CS


def shift(axis_size, step):
    return [(i, (i + step) % axis_size) for i in range(axis_size)]


def in_vmem(kernel, out_shape, scalars, arrays, name, scratch=()):
    vmem = pl.BlockSpec(memory_space=pltpu.VMEM)
    return pl.pallas_call(
        kernel,
        out_shape=out_shape,
        in_specs=[pl.BlockSpec(memory_space=pltpu.SMEM)] * len(scalars) + [vmem] * len(arrays),
        out_specs=jax.tree.map(lambda _: vmem, out_shape),
        scratch_shapes=list(scratch),
        name=name,
    )(*scalars, *arrays)


def bf16(*shape):
    return jax.ShapeDtypeStruct(shape, jnp.bfloat16)


def product(left, right):
    return jnp.dot(left, right, preferred_element_type=jnp.float32)


def product_t(left, right):
    return lax.dot_general(
        left, right, (((1,), (1,)), ((), ())), preferred_element_type=jnp.float32
    )


def norm_kernel(hid_ref, gain_ref, bias_ref, out_ref):
    inputs = hid_ref[...].astype(jnp.float32)
    average = jnp.mean(inputs, axis=1, keepdims=True)
    centered = inputs - average
    spread = jnp.mean(centered * centered, axis=1, keepdims=True)
    normed = centered / jnp.sqrt(spread + 1e-05) * gain_ref[...] + bias_ref[...]
    piece = out_ref.shape[3]
    for block in range(XS):
        for member in range(GROUP):
            first = (block * GROUP + member) * piece
            out_ref[member, block] = normed[:, first : first + piece].astype(jnp.bfloat16)


def head_lanes(head, heads):
    return pl.ds(pl.multiple_of(jnp.minimum(head, heads - 1) * HEAD, HEAD), HEAD)


def project_kernel(where_ref, in_ref, own_ref, left_ref, right_ref, far_a_ref, far_b_ref, out_ref):
    me = where_ref[0]
    parity = where_ref[1]
    members, _, rows, piece = in_ref.shape
    parts = own_ref.shape[0]
    heads = own_ref.shape[2] // HEAD
    together = 2 // parts

    def rows_of(step):
        block = lax.rem(me + step, XS)
        return in_ref[:, pl.ds(block, 1)].reshape(members * rows, piece)

    inputs = [rows_of(step) for step in (0, 3, 1, 2)]
    for first in range(0, YS, together):
        columns = [
            (part, head_lanes(CS * slot + parity, heads))
            for slot in range(first, first + together)
            for part in range(parts)
        ]

        def wide(ref):
            return jnp.concatenate([ref[part, :, lanes] for part, lanes in columns], axis=1)

        weights = [wide(own_ref), wide(left_ref), wide(right_ref)]
        weights.append(jnp.concatenate([wide(far_a_ref), wide(far_b_ref)], axis=0))
        total = product(inputs[0], weights[0])
        for left, right in zip(inputs[1:], weights[1:]):
            total += product(left, right)
        total = total.astype(jnp.bfloat16)
        width = parts * HEAD
        for index in range(together):
            out_ref[first + index] = total[:, index * width : (index + 1) * width]


def project(me_x, parity, pieces, weights):
    rows = pieces.shape[0] * pieces.shape[2]
    return in_vmem(
        project_kernel,
        bf16(YS, rows, weights[0].shape[0] * HEAD),
        [jnp.stack([me_x, parity])],
        [pieces, *weights],
        "project",
    )


def reduce_partial(me_x, me_c, pieces, weights):
    send = project(me_x, 1 - me_c, pieces, weights)
    swapped = lax.ppermute(send, "c", [(0, 1), (1, 0)])
    keep = project(me_x, me_c, pieces, weights)
    partial = (keep.astype(jnp.float32) + swapped.astype(jnp.float32)).astype(jnp.bfloat16)
    return lax.all_to_all(partial, "y", 0, 0, tiled=True)


def summed_rows(partial_ref):
    total = partial_ref[0].astype(jnp.float32)
    for source in range(1, YS):
        total += partial_ref[source].astype(jnp.float32)
    return total


def finish_kv_kernel(member_ref, partial_ref, bias_ref, out_ref):
    lanes = head_lanes(member_ref[0], bias_ref.shape[1] // HEAD)
    bias = jnp.concatenate([bias_ref[1:2, lanes], bias_ref[2:3, lanes]], axis=1)
    out_ref[...] = (summed_rows(partial_ref) + bias).astype(jnp.bfloat16)


def finish_q_kernel(tail, member_ref, partial_ref, bias_ref, out_ref, tail_ref):
    lanes = head_lanes(member_ref[0], bias_ref.shape[1] // HEAD)
    total = summed_rows(partial_ref) + bias_ref[0:1, lanes]
    queries = (total * HEAD ** (-0.5)).astype(jnp.bfloat16)
    out_ref[...] = queries
    rows = queries.shape[0] // GROUP
    for other in range(GROUP):
        last = (other + 1) * rows
        tail_ref[other] = queries[last - tail : last]


def attend_kernel(pre_dev, where_ref, query_ref, own_ref, last_ref, prior_ref, out_ref):
    odd = where_ref[0]
    start = where_ref[1]
    rows = query_ref.shape[0]
    count = rows // 4
    tok_rows = rows // GROUP
    half = pre_dev * GROUP

    def local(index):
        return (index // tok_rows) * pre_dev + index % tok_rows

    key_row = lax.broadcasted_iota(jnp.int32, (1, rows), 1)
    is_prefill = key_row % tok_rows < pre_dev
    own_pos = jnp.where(is_prefill, start + odd * half + local(key_row), FAR_AWAY)
    last_pos = jnp.where(is_prefill, start + local(key_row), FAR_AWAY)
    last_pos = jnp.where(odd == 1, last_pos, FAR_AWAY)
    old = prior_ref.shape[0] * prior_ref.shape[2]
    old_pos = lax.broadcasted_iota(jnp.int32, (1, old), 1)
    old_pos = jnp.where(old_pos < start, old_pos, FAR_AWAY)
    key_pos = jnp.concatenate([own_pos, last_pos, old_pos], axis=1)
    prior_keys = prior_ref[:, 0].reshape(old, HEAD)
    prior_values = prior_ref[:, 1].reshape(old, HEAD)
    for step in range(rows // count):
        queries = query_ref[step * count : (step + 1) * count]
        row = step * count + lax.broadcasted_iota(jnp.int32, (count, 1), 0)
        query_pos = start + odd * half + local(row)
        scores = jnp.concatenate(
            [
                product_t(queries, own_ref[:, :HEAD]),
                product_t(queries, last_ref[:, :HEAD]),
                product_t(queries, prior_keys),
            ],
            axis=1,
        )
        near = (key_pos < SINKS) | (key_pos > query_pos - WINDOW)
        scores = jnp.where((key_pos <= query_pos) & near, scores, NEG)
        highest = jnp.max(scores, axis=1, keepdims=True)
        expd = jnp.exp(scores - highest)
        totals = jnp.sum(expd, axis=1, keepdims=True)
        weights = expd.astype(jnp.bfloat16)
        weighted = (
            product(weights[:, :rows], own_ref[:, HEAD:])
            + product(weights[:, rows : 2 * rows], last_ref[:, HEAD:])
            + product(weights[:, 2 * rows :], prior_values)
        )
        out_ref[step * count : (step + 1) * count] = (weighted / totals).astype(jnp.bfloat16)


def decode_kernel(len_ref, query_ref, own_ref, cache_ref, out_ref):
    request = pl.program_id(0)
    length = len_ref[request]
    slots, _, width = cache_ref.shape[1:]
    heads = width // HEAD
    tail = query_ref.shape[1]
    row = tail - pl.num_programs(0) + request
    pick = lax.broadcasted_iota(jnp.int32, (1, tail, 1), 1) == row

    def row_of(values):
        return jnp.sum(jnp.where(pick, values.astype(jnp.float32), 0.0), axis=1)

    query = row_of(query_ref[...])
    own = row_of(own_ref[...])
    own_key, own_value = own[:, :HEAD], own[:, HEAD:]
    member = lax.broadcasted_iota(jnp.int32, (GROUP, width), 0)
    lane_head = lax.broadcasted_iota(jnp.int32, (GROUP, width), 1) // HEAD
    spread = jnp.concatenate([query] * heads, axis=1)
    spread = jnp.where(member == lane_head, spread, 0.0).astype(jnp.bfloat16)
    pairs = cache_ref[0].reshape(slots * 2, width)
    scores = product_t(spread, pairs)
    lane = lax.broadcasted_iota(jnp.int32, (1, slots * 2), 1)
    slot = lane >> 1
    near = (slot < SINKS) | (slot > length - WINDOW)
    allowed = (slot < length) & near & ((lane & 1) == 0)
    scores = jnp.where(allowed, scores, NEG)
    own_score = jnp.sum(query * own_key, axis=1, keepdims=True)
    highest = jnp.maximum(jnp.max(scores, axis=1, keepdims=True), own_score)
    expd = jnp.exp(scores - highest)
    own_expd = jnp.exp(own_score - highest)
    totals = jnp.sum(expd, axis=1, keepdims=True) + own_expd
    weights = pltpu.roll(expd, 1, 1).astype(jnp.bfloat16)
    every = product(weights, pairs)
    index = lax.broadcasted_iota(jnp.int32, (GROUP, HEAD), 0)
    weighted = own_expd.astype(jnp.bfloat16).astype(jnp.float32) * own_value
    for head in range(heads):
        lanes = every[:, head * HEAD : (head + 1) * HEAD]
        weighted += jnp.where(index == head, lanes, 0.0)
    out_ref[0] = weighted / totals


def decode(lengths, queries, own, cache):
    requests, slots, _, width = cache.shape
    tail = queries.shape[1]
    rows = own.shape[1]
    return pl.pallas_call(
        decode_kernel,
        out_shape=jax.ShapeDtypeStruct((requests, GROUP, HEAD), jnp.float32),
        grid=(requests,),
        in_specs=[
            pl.BlockSpec(memory_space=pltpu.SMEM),
            pl.BlockSpec((GROUP, tail, HEAD), lambda r: (0, 0, 0)),
            pl.BlockSpec((GROUP, tail, 2 * HEAD), lambda r: (0, rows // tail - 1, 0)),
            pl.BlockSpec((1, slots, 2, width), lambda r: (r, 0, 0, 0)),
        ],
        out_specs=pl.BlockSpec((1, GROUP, HEAD), lambda r: (r, 0, 0)),
        name="decode",
    )(lengths, queries, own, cache)


def pack_kernel(prefill_ref, decode_ref, out_ref):
    rows = prefill_ref.shape[0]
    extra = decode_ref[...].reshape(decode_ref.shape[0] * GROUP, HEAD).astype(jnp.bfloat16)
    for target in range(GROUP):
        out_ref[target, :rows] = prefill_ref[...]
        out_ref[target, rows:] = extra


def out_kernel(where_ref, in_ref, own_ref, left_ref, right_ref, far_ref, out_ref, attn_ref, w_ref):
    me = where_ref[0]
    heads = attn_ref.shape[1] // HEAD
    rows = attn_ref.shape[0]
    tok_rows = rows // GROUP
    extra = in_ref[:, rows:].astype(jnp.float32)
    requests = extra.shape[1] // GROUP
    place = lax.broadcasted_iota(jnp.int32, (1, tok_rows, 1), 1)
    for head in range(heads):
        values = in_ref[head, :rows].reshape(GROUP, tok_rows, HEAD).astype(jnp.float32)
        for request in range(requests):
            first = request * GROUP + head
            row = extra[:, first : first + 1]
            values = jnp.where(place == tok_rows - requests + request, row, values)
        values = values.astype(jnp.bfloat16).reshape(rows, HEAD)
        attn_ref[:, head * HEAD : (head + 1) * HEAD] = values
    for step, ref in ((0, own_ref), (3, left_ref), (1, right_ref), (2, far_ref)):
        w_ref[lax.rem(me + step, XS)] = ref[...]
    weights = w_ref[...].reshape(XS * w_ref.shape[1], w_ref.shape[2])
    out_ref[...] = product_t(attn_ref[...], weights).astype(jnp.bfloat16)


def final_kernel(in_ref, hid_ref, bias_ref, out_ref, row_ref):
    piece = in_ref.shape[2] // XS
    for member in range(GROUP):
        total = in_ref[member * ZS].astype(jnp.float32)
        for source in range(1, ZS):
            total += in_ref[member * ZS + source].astype(jnp.float32)
        for block in range(XS):
            first = (block * GROUP + member) * piece
            row_ref[:, first : first + piece] = total[:, block * piece : (block + 1) * piece]
    result = hid_ref[...].astype(jnp.float32) + row_ref[...] + bias_ref[...]
    result = result.astype(jnp.bfloat16)
    for target in range(ZS):
        out_ref[target] = result


def on_device(
    hidden,
    ln_gain,
    ln_bias,
    w_qkv,
    qkv_bias,
    w_out,
    out_bias,
    dec_cache,
    prior_kv,
    dec_len,
    offsets,
):
    me_x = lax.axis_index("x")
    me_c = lax.axis_index("c")
    me_z = lax.axis_index("z")
    member = lax.axis_index("y") * CS + me_c
    tok_rows, width = hidden.shape
    dec_dev = dec_cache.shape[0]
    pre_dev = tok_rows - dec_dev
    head_width = w_qkv.shape[2]
    heads = head_width // HEAD
    pcb = prior_kv.shape[0]
    rows = GROUP * tok_rows
    start = jnp.where(me_x // 2 == 0, offsets[0], offsets[1])
    half = w_qkv.shape[0] // 2
    tail = 16

    turned = w_qkv.transpose(1, 0, 2)
    kv_own, q_own = turned[1:], turned[:1]
    kv_left = lax.ppermute(kv_own, "x", shift(XS, 1))
    kv_right = lax.ppermute(kv_own, "x", shift(XS, -1))
    kv_left, kv_right, q_own = lax.optimization_barrier((kv_left, kv_right, q_own))
    kv_far_a = lax.ppermute(kv_left[:, :half], "x", shift(XS, 1))
    kv_far_b = lax.ppermute(kv_right[:, half:], "x", shift(XS, -1))
    q_left = lax.ppermute(q_own, "x", shift(XS, 1))
    q_right = lax.ppermute(q_own, "x", shift(XS, -1))
    q_far_a = lax.ppermute(q_left[:, :half], "x", shift(XS, 1))
    q_far_b = lax.ppermute(q_right[:, half:], "x", shift(XS, -1))

    pieces = in_vmem(
        norm_kernel,
        bf16(GROUP, XS, tok_rows, width // (XS * GROUP)),
        [],
        [hidden, ln_gain[None], ln_bias[None]],
        "norm",
    )
    pieces = lax.all_to_all(pieces, ("y", "c"), 0, 0, tiled=True)

    prior = prior_kv.reshape(pcb, 2, 2, heads, HEAD)
    prior = jnp.pad(prior, ((0, 0), (0, 0), (0, 0), (0, GROUP - heads), (0, 0)))
    prior = prior.transpose(1, 3, 2, 0, 4)
    prior = jnp.repeat(prior, 2, axis=0).reshape(XS * GROUP, 2, pcb, HEAD)
    pieces, prior = lax.optimization_barrier((pieces, prior))
    prior = lax.all_to_all(prior, ("x", "y", "c"), 0, 0, tiled=True)

    where = member[None]
    kv_parts = reduce_partial(
        me_x, me_c, pieces, (kv_own, kv_left, kv_right, kv_far_a, kv_far_b)
    )
    own_kv = in_vmem(
        finish_kv_kernel, bf16(rows, 2 * HEAD), [where], [kv_parts, qkv_bias], "finish_kv"
    )
    last_kv = lax.ppermute(own_kv, "x", [(0, 1), (2, 3)])
    mine = lax.all_to_all(
        own_kv.reshape(GROUP, tok_rows, 2 * HEAD), ("y", "c"), 0, 0, tiled=True
    )
    new_kv = mine[:heads].reshape(heads, tok_rows, 2, HEAD)
    new_kv = new_kv.transpose(1, 2, 0, 3).reshape(tok_rows, 2, head_width)

    q_far_a, q_far_b, prior, w_out = lax.optimization_barrier((q_far_a, q_far_b, prior, w_out))
    q_parts = reduce_partial(me_x, me_c, pieces, (q_own, q_left, q_right, q_far_a, q_far_b))
    w_own = w_out.T
    w_left = lax.ppermute(w_own, "x", shift(XS, 1))
    w_right = lax.ppermute(w_own, "x", shift(XS, -1))
    w_far = lax.ppermute(w_own, "x", shift(XS, 2))

    queries, ends = in_vmem(
        functools.partial(finish_q_kernel, tail),
        (bf16(rows, HEAD), bf16(GROUP, tail, HEAD)),
        [where],
        [q_parts, qkv_bias],
        "finish_q",
    )
    ends = lax.all_to_all(ends, ("y", "c"), 0, 0, tiled=True)
    prefilled = in_vmem(
        functools.partial(attend_kernel, pre_dev),
        bf16(rows, HEAD),
        [jnp.stack([me_x % 2, start])],
        [queries, own_kv, last_kv, prior],
        "attend",
    )
    decoded = decode(dec_len, ends, mine, dec_cache)
    payload = in_vmem(
        pack_kernel,
        bf16(GROUP, rows + dec_dev * GROUP, HEAD),
        [],
        [prefilled, decoded],
        "pack",
    )
    payload, w_left, w_right, w_far = lax.optimization_barrier((payload, w_left, w_right, w_far))
    gathered = lax.all_to_all(payload, ("y", "c"), 0, 0, tiled=True)
    piece = w_own.shape[0]
    shares = in_vmem(
        out_kernel,
        bf16(rows, XS * piece),
        [me_x[None]],
        [gathered, w_own, w_left, w_right, w_far],
        "out",
        [
            pltpu.VMEM((rows, head_width), jnp.bfloat16),
            pltpu.VMEM((XS, piece, head_width), jnp.bfloat16),
        ],
    )
    slab = tok_rows // ZS
    shares = shares.reshape(GROUP * ZS, slab, XS * piece)
    shares = lax.all_to_all(shares, ("y", "c", "z"), 0, 0, tiled=True)
    residual = lax.dynamic_slice(hidden, (me_z * slab, 0), (slab, width))
    result = in_vmem(
        final_kernel,
        bf16(ZS, slab, width),
        [],
        [shares, residual, out_bias[None]],
        "final",
        [pltpu.VMEM((slab, width), jnp.float32)],
    )
    result = lax.all_to_all(result, "z", 0, 0, tiled=True).reshape(tok_rows, width)
    return (result, new_kv)


def solution(mesh):
    fine = Mesh(mesh.devices.reshape(XS, YS, CS, ZS), ("x", "y", "c", "z"))
    tok = ("x", "y", "c")
    in_specs = (
        P(tok, None),
        P(),
        P(),
        P(tok, None, "z"),
        P(None, "z"),
        P("z", tok),
        P(),
        P(tok, None, None, "z"),
        P(tok, None, None, "z"),
        P(tok),
        P(),
    )
    out_specs = (P(tok, None), P(tok, None, "z"))
    return jax.shard_map(
        on_device, mesh=fine, in_specs=in_specs, out_specs=out_specs, check_vma=False
    )
```

```python
import functools

import jax
import jax.numpy as jnp
from jax import lax
from jax.experimental import pallas as pl
from jax.experimental.pallas import tpu as pltpu
from jax.sharding import Mesh, PartitionSpec as P


HEAD = 128
WINDOW = 512
SINKS = 4
NEG = -1e30
FAR_AWAY = 1 << 20
SMALL_VMEM = 16 << 20
XS, YS, CS, ZS = 4, 4, 2, 8
GROUP = YS * CS


def shift(axis_size, step):
    return [(i, (i + step) % axis_size) for i in range(axis_size)]


def in_vmem(kernel, out_shape, scalars, arrays, scratch=()):
    vmem = pl.BlockSpec(memory_space=pltpu.VMEM)
    return pl.pallas_call(
        kernel,
        out_shape=out_shape,
        in_specs=[pl.BlockSpec(memory_space=pltpu.SMEM)] * len(scalars) + [vmem] * len(arrays),
        out_specs=jax.tree.map(lambda _: vmem, out_shape),
        scratch_shapes=list(scratch),
        compiler_params=pltpu.CompilerParams(vmem_limit_bytes=SMALL_VMEM),
    )(*scalars, *[pltpu.with_memory_space_constraint(a, pltpu.VMEM) for a in arrays])


def bf16(*shape):
    return jax.ShapeDtypeStruct(shape, jnp.bfloat16)


def product(left, right):
    return jnp.dot(left, right, preferred_element_type=jnp.float32)


def product_t(left, right):
    return lax.dot_general(
        left, right, (((1,), (1,)), ((), ())), preferred_element_type=jnp.float32
    )


def norm_kernel(hid_ref, gain_ref, bias_ref, out_ref):
    inputs = hid_ref[...].astype(jnp.float32)
    average = jnp.mean(inputs, axis=1, keepdims=True)
    centered = inputs - average
    spread = jnp.mean(centered * centered, axis=1, keepdims=True)
    normed = centered / jnp.sqrt(spread + 1e-05) * gain_ref[...] + bias_ref[...]
    piece = out_ref.shape[3]
    for block in range(XS):
        for member in range(GROUP):
            first = (block * GROUP + member) * piece
            out_ref[member, block] = normed[:, first : first + piece].astype(jnp.bfloat16)


def head_lanes(head, heads):
    return pl.ds(pl.multiple_of(jnp.minimum(head, heads - 1) * HEAD, HEAD), HEAD)


def project_kernel(with_extra, where_ref, *refs):
    if with_extra:
        in_ref, own_ref, left_ref, right_ref, far_a_ref, far_b_ref, more_ref = refs[:7]
    else:
        in_ref, own_ref, left_ref, right_ref, far_a_ref, far_b_ref = refs[:6]
    send_ref, keep_ref, extra_ref = refs[-3:]
    me = where_ref[0]
    core = where_ref[1]
    members, _, tok_rows, piece = in_ref.shape
    rows = members * tok_rows
    parts = own_ref.shape[0]
    heads = own_ref.shape[2] // HEAD
    together = 2 // parts
    width = parts * HEAD
    requests = extra_ref.shape[1] // (parts * GROUP)

    def rows_of(step):
        block = lax.rem(me + step, XS)
        return in_ref[:, pl.ds(block, 1)].reshape(rows, piece)

    inputs = [rows_of(step) for step in (0, 3, 1, 2)]
    for side, out_ref in ((1 - core, send_ref), (core, keep_ref)):
        for first in range(0, YS, together):
            slots = list(range(first, first + together))
            columns = [
                (part, head_lanes(CS * slot + side, heads))
                for slot in slots
                for part in range(parts)
            ]

            def wide(ref):
                return jnp.concatenate([ref[part, :, lanes] for part, lanes in columns], axis=1)

            weights = [wide(own_ref), wide(left_ref), wide(right_ref)]
            weights.append(jnp.concatenate([wide(far_a_ref), wide(far_b_ref)], axis=0))
            total = product(inputs[0], weights[0])
            for left, right in zip(inputs[1:], weights[1:]):
                total += product(left, right)
            for index, slot in enumerate(slots):
                mine = total[:, index * width : (index + 1) * width]
                out_ref[slot, :rows] = mine.astype(jnp.bfloat16)
                by_member = mine.reshape(members, tok_rows, width)
                for request in range(requests):
                    row = by_member[:, tok_rows - requests + request]
                    for part in range(parts):
                        place = (request * parts + part) * GROUP + CS * slot + side
                        extra_ref[:, pl.ds(place, 1)] = row[:, None, part * HEAD : (part + 1) * HEAD]
    if with_extra:
        for side, out_ref in ((1 - core, send_ref), (core, keep_ref)):
            for slot in range(YS):
                member = CS * slot + side
                for request in range(requests):
                    query = extra_ref[member, request * GROUP : (request + 1) * GROUP]
                    pair = more_ref[member, request * 2 * GROUP : (request + 1) * 2 * GROUP]
                    block = jnp.concatenate([query, pair], axis=0).astype(jnp.bfloat16)
                    if request == 0:
                        blocks = [block]
                    else:
                        blocks.append(block)
                out_ref[slot, rows:] = jnp.concatenate(blocks, axis=0)


def project(me_x, me_c, requests, pieces, weights, more=None):
    rows = pieces.shape[0] * pieces.shape[2]
    parts = weights[0].shape[0]
    extra = 0 if more is None else 3 * GROUP * requests
    out = bf16(YS, rows + extra, parts * HEAD)
    kept = jax.ShapeDtypeStruct((GROUP, parts * GROUP * requests, HEAD), jnp.float32)
    return in_vmem(
        functools.partial(project_kernel, more is not None),
        (out, out, kept),
        [jnp.stack([me_x, me_c])],
        [pieces, *weights] + ([] if more is None else [more]),
    )


def add_kernel(left_ref, right_ref, out_ref):
    total = left_ref[...].astype(jnp.float32) + right_ref[...].astype(jnp.float32)
    out_ref[...] = total.astype(jnp.bfloat16)


def reduce_partial(send, keep):
    swapped = lax.ppermute(send, "c", [(0, 1), (1, 0)])
    partial = in_vmem(add_kernel, bf16(*keep.shape), [], [keep, swapped])
    return lax.all_to_all(partial, "y", 0, 0, tiled=True)


def summed_rows(partial_ref):
    total = partial_ref[0].astype(jnp.float32)
    for source in range(1, YS):
        total += partial_ref[source].astype(jnp.float32)
    return total


def finish_kv_kernel(member_ref, partial_ref, bias_ref, out_ref):
    lanes = head_lanes(member_ref[0], bias_ref.shape[1] // HEAD)
    bias = jnp.concatenate([bias_ref[1:2, lanes], bias_ref[2:3, lanes]], axis=1)
    out_ref[...] = (summed_rows(partial_ref) + bias).astype(jnp.bfloat16)


def finish_q_kernel(member_ref, partial_ref, bias_ref, out_ref, decode_ref):
    lanes = head_lanes(member_ref[0], bias_ref.shape[1] // HEAD)
    total = summed_rows(partial_ref)
    rows = out_ref.shape[0]
    queries = (total[:rows] + bias_ref[0:1, lanes]) * HEAD ** (-0.5)
    out_ref[...] = queries.astype(jnp.bfloat16)
    decode_ref[...] = total[rows:]


def attend_kernel(pre_dev, where_ref, query_ref, own_ref, last_ref, prior_ref, out_ref):
    odd = where_ref[0]
    start = where_ref[1]
    rows = query_ref.shape[0]
    count = rows // 4
    tok_rows = rows // GROUP
    half = pre_dev * GROUP

    def local(index):
        return (index // tok_rows) * pre_dev + index % tok_rows

    key_row = lax.broadcasted_iota(jnp.int32, (1, rows), 1)
    is_prefill = key_row % tok_rows < pre_dev
    own_pos = jnp.where(is_prefill, start + odd * half + local(key_row), FAR_AWAY)
    last_pos = jnp.where(is_prefill, start + local(key_row), FAR_AWAY)
    last_pos = jnp.where(odd == 1, last_pos, FAR_AWAY)
    old = prior_ref.shape[0] * prior_ref.shape[2]
    old_pos = lax.broadcasted_iota(jnp.int32, (1, old), 1)
    old_pos = jnp.where(old_pos < start, old_pos, FAR_AWAY)
    key_pos = jnp.concatenate([own_pos, last_pos, old_pos], axis=1)
    prior_keys = prior_ref[:, 0].reshape(old, HEAD)
    prior_values = prior_ref[:, 1].reshape(old, HEAD)
    for step in range(rows // count):
        queries = query_ref[step * count : (step + 1) * count]
        row = step * count + lax.broadcasted_iota(jnp.int32, (count, 1), 0)
        query_pos = start + odd * half + local(row)
        scores = jnp.concatenate(
            [
                product_t(queries, own_ref[:, :HEAD]),
                product_t(queries, last_ref[:, :HEAD]),
                product_t(queries, prior_keys),
            ],
            axis=1,
        )
        near = (key_pos < SINKS) | (key_pos > query_pos - WINDOW)
        scores = jnp.where((key_pos <= query_pos) & near, scores, NEG)
        highest = jnp.max(scores, axis=1, keepdims=True)
        expd = jnp.exp(scores - highest)
        totals = jnp.sum(expd, axis=1, keepdims=True)
        weights = expd.astype(jnp.bfloat16)
        weighted = (
            product(weights[:, :rows], own_ref[:, HEAD:])
            + product(weights[:, rows : 2 * rows], last_ref[:, HEAD:])
            + product(weights[:, 2 * rows :], prior_values)
        )
        out_ref[step * count : (step + 1) * count] = (weighted / totals).astype(jnp.bfloat16)


def decode_kernel(len_ref, sums_ref, bias_ref, cache_ref, out_ref):
    request = pl.program_id(0)
    length = len_ref[request]
    slots, _, width = cache_ref.shape[1:]
    heads = width // HEAD

    def rounded(part, factor):
        total = (sums_ref[part * GROUP : (part + 1) * GROUP] + bias_ref[part]) * factor
        return total.astype(jnp.bfloat16).astype(jnp.float32)

    query = rounded(0, HEAD ** (-0.5))
    own_key, own_value = rounded(1, 1.0), rounded(2, 1.0)
    member = lax.broadcasted_iota(jnp.int32, (GROUP, width), 0)
    lane_head = lax.broadcasted_iota(jnp.int32, (GROUP, width), 1) // HEAD
    spread = jnp.concatenate([query] * heads, axis=1)
    spread = jnp.where(member == lane_head, spread, 0.0).astype(jnp.bfloat16)
    pairs = cache_ref[0].reshape(slots * 2, width)
    scores = product_t(spread, pairs)
    lane = lax.broadcasted_iota(jnp.int32, (1, slots * 2), 1)
    slot = lane >> 1
    near = (slot < SINKS) | (slot > length - WINDOW)
    allowed = (slot < length) & near & ((lane & 1) == 0)
    scores = jnp.where(allowed, scores, NEG)
    own_score = jnp.sum(query * own_key, axis=1, keepdims=True)
    highest = jnp.maximum(jnp.max(scores, axis=1, keepdims=True), own_score)
    expd = jnp.exp(scores - highest)
    own_expd = jnp.exp(own_score - highest)
    totals = jnp.sum(expd, axis=1, keepdims=True) + own_expd
    weights = pltpu.roll(expd, 1, 1).astype(jnp.bfloat16)
    every = product(weights, pairs)
    index = lax.broadcasted_iota(jnp.int32, (GROUP, HEAD), 0)
    weighted = own_expd.astype(jnp.bfloat16).astype(jnp.float32) * own_value
    for head in range(heads):
        lanes = every[:, head * HEAD : (head + 1) * HEAD]
        weighted += jnp.where(index == head, lanes, 0.0)
    out_ref[0] = weighted / totals


def decode(lengths, sums, bias, cache):
    requests, slots, _, width = cache.shape
    return pl.pallas_call(
        decode_kernel,
        out_shape=jax.ShapeDtypeStruct((requests, GROUP, HEAD), jnp.float32),
        grid=(requests,),
        in_specs=[
            pl.BlockSpec(memory_space=pltpu.SMEM),
            pl.BlockSpec((3 * GROUP, HEAD), lambda r: (r, 0)),
            pl.BlockSpec(bias.shape, lambda r: (0, 0, 0)),
            pl.BlockSpec((1, slots, 2, width), lambda r: (r, 0, 0, 0)),
        ],
        out_specs=pl.BlockSpec((1, GROUP, HEAD), lambda r: (r, 0, 0)),
        compiler_params=pltpu.CompilerParams(vmem_limit_bytes=2 * SMALL_VMEM),
        name="decode",
    )(lengths, sums, bias, cache)


def pack_kernel(prefill_ref, decode_ref, out_ref):
    rows = prefill_ref.shape[0]
    extra = decode_ref[...].reshape(decode_ref.shape[0] * GROUP, HEAD).astype(jnp.bfloat16)
    for target in range(GROUP):
        out_ref[target, :rows] = prefill_ref[...]
        out_ref[target, rows:] = extra


def out_kernel(where_ref, in_ref, own_ref, left_ref, right_ref, far_ref, out_ref, attn_ref, w_ref):
    me = where_ref[0]
    heads = attn_ref.shape[1] // HEAD
    rows = attn_ref.shape[0]
    tok_rows = rows // GROUP
    extra = in_ref[:, rows:].astype(jnp.float32)
    requests = extra.shape[1] // GROUP
    place = lax.broadcasted_iota(jnp.int32, (1, tok_rows, 1), 1)
    for head in range(heads):
        values = in_ref[head, :rows].reshape(GROUP, tok_rows, HEAD).astype(jnp.float32)
        for request in range(requests):
            first = request * GROUP + head
            row = extra[:, first : first + 1]
            values = jnp.where(place == tok_rows - requests + request, row, values)
        values = values.astype(jnp.bfloat16).reshape(rows, HEAD)
        attn_ref[:, head * HEAD : (head + 1) * HEAD] = values
    for step, ref in ((0, own_ref), (3, left_ref), (1, right_ref), (2, far_ref)):
        w_ref[lax.rem(me + step, XS)] = ref[...]
    weights = w_ref[...].reshape(XS * w_ref.shape[1], w_ref.shape[2])
    out_ref[...] = product_t(attn_ref[...], weights).astype(jnp.bfloat16)


def final_kernel(in_ref, hid_ref, bias_ref, out_ref, row_ref):
    piece = in_ref.shape[2] // XS
    for member in range(GROUP):
        total = in_ref[member * ZS].astype(jnp.float32)
        for source in range(1, ZS):
            total += in_ref[member * ZS + source].astype(jnp.float32)
        for block in range(XS):
            first = (block * GROUP + member) * piece
            row_ref[:, first : first + piece] = total[:, block * piece : (block + 1) * piece]
    result = hid_ref[...].astype(jnp.float32) + row_ref[...] + bias_ref[...]
    result = result.astype(jnp.bfloat16)
    for target in range(ZS):
        out_ref[target] = result


def on_device(
    hidden,
    ln_gain,
    ln_bias,
    w_qkv,
    qkv_bias,
    w_out,
    out_bias,
    dec_cache,
    prior_kv,
    dec_len,
    offsets,
):
    me_x = lax.axis_index("x")
    me_c = lax.axis_index("c")
    me_z = lax.axis_index("z")
    member = lax.axis_index("y") * CS + me_c
    tok_rows, width = hidden.shape
    dec_dev = dec_cache.shape[0]
    pre_dev = tok_rows - dec_dev
    head_width = w_qkv.shape[2]
    heads = head_width // HEAD
    pcb = prior_kv.shape[0]
    rows = GROUP * tok_rows
    start = jnp.where(me_x // 2 == 0, offsets[0], offsets[1])
    half = w_qkv.shape[0] // 2

    turned = w_qkv.transpose(1, 0, 2)
    kv_own, q_own = turned[1:], turned[:1]
    kv_left = lax.ppermute(kv_own, "x", shift(XS, 1))
    kv_right = lax.ppermute(kv_own, "x", shift(XS, -1))
    kv_left, kv_right, q_own = lax.optimization_barrier((kv_left, kv_right, q_own))
    kv_far_a = lax.ppermute(kv_left[:, :half], "x", shift(XS, 1))
    kv_far_b = lax.ppermute(kv_right[:, half:], "x", shift(XS, -1))
    q_left = lax.ppermute(q_own, "x", shift(XS, 1))
    q_right = lax.ppermute(q_own, "x", shift(XS, -1))
    q_far_a = lax.ppermute(q_left[:, :half], "x", shift(XS, 1))
    q_far_b = lax.ppermute(q_right[:, half:], "x", shift(XS, -1))

    pieces = in_vmem(
        norm_kernel,
        bf16(GROUP, XS, tok_rows, width // (XS * GROUP)),
        [],
        [hidden, ln_gain[None], ln_bias[None]],
    )
    pieces = lax.all_to_all(pieces, ("y", "c"), 0, 0, tiled=True)

    prior = prior_kv.reshape(pcb, 2, 2, heads, HEAD)
    prior = jnp.pad(prior, ((0, 0), (0, 0), (0, 0), (0, GROUP - heads), (0, 0)))
    prior = prior.transpose(1, 3, 2, 0, 4)
    prior = jnp.repeat(prior, 2, axis=0).reshape(XS * GROUP, 2, pcb, HEAD)
    pieces, prior = lax.optimization_barrier((pieces, prior))
    prior = lax.all_to_all(prior, ("x", "y", "c"), 0, 0, tiled=True)

    where = member[None]
    kv_send, kv_keep, kv_extra = project(
        me_x, me_c, dec_dev, pieces, (kv_own, kv_left, kv_right, kv_far_a, kv_far_b)
    )
    kv_keep, prior = lax.optimization_barrier((kv_keep, prior))
    kv_parts = reduce_partial(kv_send, kv_keep)
    own_kv = in_vmem(finish_kv_kernel, bf16(rows, 2 * HEAD), [where], [kv_parts, qkv_bias])
    last_kv = lax.ppermute(own_kv, "x", [(0, 1), (2, 3)])

    q_far_a, q_far_b, w_out = lax.optimization_barrier((q_far_a, q_far_b, w_out))
    q_send, q_keep, _ = project(
        me_x, me_c, dec_dev, pieces, (q_own, q_left, q_right, q_far_a, q_far_b), kv_extra
    )
    q_parts = reduce_partial(q_send, q_keep)
    w_own = w_out.T
    w_left = lax.ppermute(w_own, "x", shift(XS, 1))
    w_right = lax.ppermute(w_own, "x", shift(XS, -1))
    w_far = lax.ppermute(w_own, "x", shift(XS, 2))

    queries, sums = in_vmem(
        finish_q_kernel,
        (
            bf16(rows, HEAD),
            jax.ShapeDtypeStruct((3 * GROUP * dec_dev, HEAD), jnp.float32),
        ),
        [where],
        [q_parts, qkv_bias],
    )
    tied_kv, queries = lax.optimization_barrier((own_kv, queries))
    mine = lax.all_to_all(tied_kv.reshape(GROUP, tok_rows, 2 * HEAD), ("y", "c"), 0, 0, tiled=True)
    new_kv = mine[:heads].reshape(heads, tok_rows, 2, HEAD)
    new_kv = new_kv.transpose(1, 2, 0, 3).reshape(tok_rows, 2, head_width)
    prefilled = in_vmem(
        functools.partial(attend_kernel, pre_dev),
        bf16(rows, HEAD),
        [jnp.stack([me_x % 2, start])],
        [queries, own_kv, last_kv, prior],
    )
    head_bias = jnp.pad(qkv_bias.reshape(3, heads, HEAD), ((0, 0), (0, GROUP - heads), (0, 0)))
    decoded = decode(dec_len, sums, head_bias, dec_cache)
    payload = in_vmem(
        pack_kernel, bf16(GROUP, rows + dec_dev * GROUP, HEAD), [], [prefilled, decoded]
    )
    payload, new_kv, w_left, w_right, w_far = lax.optimization_barrier(
        (payload, new_kv, w_left, w_right, w_far)
    )
    gathered = lax.all_to_all(payload, ("y", "c"), 0, 0, tiled=True)
    piece = w_own.shape[0]
    shares = in_vmem(
        out_kernel,
        bf16(rows, XS * piece),
        [me_x[None]],
        [gathered, w_own, w_left, w_right, w_far],
        [
            pltpu.VMEM((rows, head_width), jnp.bfloat16),
            pltpu.VMEM((XS, piece, head_width), jnp.bfloat16),
        ],
    )
    slab = tok_rows // ZS
    shares = shares.reshape(GROUP * ZS, slab, XS * piece)
    shares = lax.all_to_all(shares, ("y", "c", "z"), 0, 0, tiled=True)
    residual = lax.dynamic_slice(hidden, (me_z * slab, 0), (slab, width))
    result = in_vmem(
        final_kernel,
        bf16(ZS, slab, width),
        [],
        [shares, residual, out_bias[None]],
        [pltpu.VMEM((slab, width), jnp.float32)],
    )
    result = lax.all_to_all(result, "z", 0, 0, tiled=True).reshape(tok_rows, width)
    return (result, new_kv)


def solution(mesh):
    fine = Mesh(mesh.devices.reshape(XS, YS, CS, ZS), ("x", "y", "c", "z"))
    tok = ("x", "y", "c")
    in_specs = (
        P(tok, None),
        P(),
        P(),
        P(tok, None, "z"),
        P(None, "z"),
        P("z", tok),
        P(),
        P(tok, None, None, "z"),
        P(tok, None, None, "z"),
        P(tok),
        P(),
    )
    out_specs = (P(tok, None), P(tok, None, "z"))

    return jax.shard_map(
        on_device, mesh=fine, in_specs=in_specs, out_specs=out_specs, check_vma=False
    )
```

```python
import functools

import jax
import jax.numpy as jnp
from jax import lax
from jax.experimental import pallas as pl
from jax.experimental.pallas import tpu as pltpu
from jax.sharding import Mesh, PartitionSpec as P


HEAD = 128
WINDOW = 512
SINKS = 4
NEG = -1e30
FAR_AWAY = 1 << 20
SMALL_VMEM = 16 << 20
XS, YS, CS, ZS = 4, 4, 2, 8
GROUP = YS * CS


def shift(axis_size, step):
    return [(i, (i + step) % axis_size) for i in range(axis_size)]


def in_vmem(kernel, out_shape, scalars, arrays, scratch=()):
    vmem = pl.BlockSpec(memory_space=pltpu.VMEM)
    return pl.pallas_call(
        kernel,
        out_shape=out_shape,
        in_specs=[pl.BlockSpec(memory_space=pltpu.SMEM)] * len(scalars) + [vmem] * len(arrays),
        out_specs=jax.tree.map(lambda _: vmem, out_shape),
        scratch_shapes=list(scratch),
        compiler_params=pltpu.CompilerParams(vmem_limit_bytes=SMALL_VMEM),
    )(*scalars, *[pltpu.with_memory_space_constraint(a, pltpu.VMEM) for a in arrays])


def bf16(*shape):
    return jax.ShapeDtypeStruct(shape, jnp.bfloat16)


def product(left, right):
    return jnp.dot(left, right, preferred_element_type=jnp.float32)


def product_t(left, right):
    return lax.dot_general(
        left, right, (((1,), (1,)), ((), ())), preferred_element_type=jnp.float32
    )


def norm_kernel(hid_ref, gain_ref, bias_ref, prior_ref, out_ref):
    inputs = hid_ref[...].astype(jnp.float32)
    rows = inputs.shape[0]
    average = jnp.mean(inputs, axis=1, keepdims=True)
    centered = inputs - average
    spread = jnp.mean(centered * centered, axis=1, keepdims=True)
    normed = centered / jnp.sqrt(spread + 1e-05) * gain_ref[...] + bias_ref[...]
    piece = out_ref.shape[3]
    heads = prior_ref.shape[3] // HEAD
    for block in range(XS):
        earlier = prior_ref[:, block // 2, block % 2]
        for member in range(GROUP):
            first = (block * GROUP + member) * piece
            out_ref[member, block, :rows] = normed[:, first : first + piece].astype(jnp.bfloat16)
            head = min(member, heads - 1)
            out_ref[member, block, rows:, :HEAD] = earlier[:, head * HEAD : (head + 1) * HEAD]


def my_member():
    return lax.axis_index("y") * CS + lax.axis_index("c")


def turned_x(step):
    return lax.rem(lax.axis_index("x") + step, XS)


def split_kernel(in_ref, *out_refs):
    rows = in_ref.shape[2] - out_refs[0].shape[2]
    for step, out_ref in zip((0, 1, 3, 2), out_refs):
        request = turned_x(step) // 2
        out_ref[...] = in_ref[:, pl.ds(request * 2, 2), rows:, :HEAD]


def head_lanes(head, heads):
    return pl.ds(pl.multiple_of(jnp.minimum(head, heads - 1) * HEAD, HEAD), HEAD)


def project_kernel(with_extra, tok_rows, *refs):
    if with_extra:
        in_ref, own_ref, left_ref, right_ref, far_a_ref, far_b_ref, more_ref = refs[:7]
    else:
        in_ref, own_ref, left_ref, right_ref, far_a_ref, far_b_ref = refs[:6]
    send_ref, keep_ref, extra_ref = refs[-3:]
    core = lax.axis_index("c")
    members, piece = in_ref.shape[0], in_ref.shape[3]
    rows = members * tok_rows
    parts = own_ref.shape[0]
    heads = own_ref.shape[2] // HEAD
    together = 2 // parts
    width = parts * HEAD
    requests = extra_ref.shape[1] // (parts * GROUP)

    def rows_of(step):
        return in_ref[:, pl.ds(turned_x(step), 1), :tok_rows].reshape(rows, piece)

    inputs = [rows_of(step) for step in (0, 3, 1, 2)]
    for side, out_ref in ((1 - core, send_ref), (core, keep_ref)):
        for first in range(0, YS, together):
            slots = list(range(first, first + together))
            columns = [
                (part, head_lanes(CS * slot + side, heads))
                for slot in slots
                for part in range(parts)
            ]

            def wide(ref):
                return jnp.concatenate([ref[part, :, lanes] for part, lanes in columns], axis=1)

            weights = [wide(own_ref), wide(left_ref), wide(right_ref)]
            weights.append(jnp.concatenate([wide(far_a_ref), wide(far_b_ref)], axis=0))
            total = product(inputs[0], weights[0])
            for left, right in zip(inputs[1:], weights[1:]):
                total += product(left, right)
            for index, slot in enumerate(slots):
                mine = total[:, index * width : (index + 1) * width]
                out_ref[slot, :rows] = mine.astype(jnp.bfloat16)
                by_member = mine.reshape(members, tok_rows, width)
                for request in range(requests):
                    row = by_member[:, tok_rows - requests + request]
                    for part in range(parts):
                        place = (request * parts + part) * GROUP + CS * slot + side
                        extra_ref[:, pl.ds(place, 1)] = row[:, None, part * HEAD : (part + 1) * HEAD]
    if with_extra:
        for side, out_ref in ((1 - core, send_ref), (core, keep_ref)):
            for slot in range(YS):
                member = CS * slot + side
                for request in range(requests):
                    query = extra_ref[member, request * GROUP : (request + 1) * GROUP]
                    pair = more_ref[member, request * 2 * GROUP : (request + 1) * 2 * GROUP]
                    block = jnp.concatenate([query, pair], axis=0).astype(jnp.bfloat16)
                    if request == 0:
                        blocks = [block]
                    else:
                        blocks.append(block)
                out_ref[slot, rows:] = jnp.concatenate(blocks, axis=0)


def project(tok_rows, requests, pieces, weights, more=None):
    rows = pieces.shape[0] * tok_rows
    parts = weights[0].shape[0]
    extra = 0 if more is None else 3 * GROUP * requests
    out = bf16(YS, rows + extra, parts * HEAD)
    kept = jax.ShapeDtypeStruct((GROUP, parts * GROUP * requests, HEAD), jnp.float32)
    return in_vmem(
        functools.partial(project_kernel, more is not None, tok_rows),
        (out, out, kept),
        [],
        [pieces, *weights] + ([] if more is None else [more]),
    )


def add_kernel(left_ref, right_ref, out_ref):
    total = left_ref[...].astype(jnp.float32) + right_ref[...].astype(jnp.float32)
    out_ref[...] = total.astype(jnp.bfloat16)


def reduce_partial(send, keep):
    swapped = lax.ppermute(send, "c", [(0, 1), (1, 0)])
    partial = in_vmem(add_kernel, bf16(*keep.shape), [], [keep, swapped])
    return lax.all_to_all(partial, "y", 0, 0, tiled=True)


def summed_rows(partial_ref):
    total = partial_ref[0].astype(jnp.float32)
    for source in range(1, YS):
        total += partial_ref[source].astype(jnp.float32)
    return total


def finish_kv_kernel(partial_ref, bias_ref, out_ref):
    lanes = head_lanes(my_member(), bias_ref.shape[1] // HEAD)
    bias = jnp.concatenate([bias_ref[1:2, lanes], bias_ref[2:3, lanes]], axis=1)
    out_ref[...] = (summed_rows(partial_ref) + bias).astype(jnp.bfloat16)


def finish_q_kernel(partial_ref, bias_ref, out_ref, decode_ref):
    lanes = head_lanes(my_member(), bias_ref.shape[1] // HEAD)
    total = summed_rows(partial_ref)
    rows = out_ref.shape[0]
    queries = (total[:rows] + bias_ref[0:1, lanes]) * HEAD ** (-0.5)
    out_ref[...] = queries.astype(jnp.bfloat16)
    decode_ref[...] = total[rows:]


def attend_kernel(pre_dev, offset_ref, query_ref, own_ref, last_ref, *refs):
    prior_refs, out_ref = refs[:-1], refs[-1]
    odd = lax.axis_index("x") % 2
    start = offset_ref[lax.axis_index("x") // 2]
    rows = query_ref.shape[0]
    count = rows // 4
    tok_rows = rows // GROUP
    half = pre_dev * GROUP

    def local(index):
        return (index // tok_rows) * pre_dev + index % tok_rows

    key_row = lax.broadcasted_iota(jnp.int32, (1, rows), 1)
    is_prefill = key_row % tok_rows < pre_dev
    own_pos = jnp.where(is_prefill, start + odd * half + local(key_row), FAR_AWAY)
    last_pos = jnp.where(is_prefill, start + local(key_row), FAR_AWAY)
    last_pos = jnp.where(odd == 1, last_pos, FAR_AWAY)
    old = prior_refs[0].shape[0] * prior_refs[0].shape[2]
    near_old = lax.broadcasted_iota(jnp.int32, (1, old), 1)
    old_pos = jnp.concatenate([turned_x(step) * old + near_old for step in (0, 3, 1, 2)], axis=1)
    old_pos = jnp.where(old_pos < start, old_pos, FAR_AWAY)
    key_pos = jnp.concatenate([own_pos, last_pos, old_pos], axis=1)
    prior_keys = jnp.concatenate([ref[:, 0].reshape(old, HEAD) for ref in prior_refs], axis=0)
    prior_values = jnp.concatenate([ref[:, 1].reshape(old, HEAD) for ref in prior_refs], axis=0)
    for step in range(rows // count):
        queries = query_ref[step * count : (step + 1) * count]
        row = step * count + lax.broadcasted_iota(jnp.int32, (count, 1), 0)
        query_pos = start + odd * half + local(row)
        scores = jnp.concatenate(
            [
                product_t(queries, own_ref[:, :HEAD]),
                product_t(queries, last_ref[:, :HEAD]),
                product_t(queries, prior_keys),
            ],
            axis=1,
        )
        near = (key_pos < SINKS) | (key_pos > query_pos - WINDOW)
        scores = jnp.where((key_pos <= query_pos) & near, scores, NEG)
        highest = jnp.max(scores, axis=1, keepdims=True)
        expd = jnp.exp(scores - highest)
        totals = jnp.sum(expd, axis=1, keepdims=True)
        weights = expd.astype(jnp.bfloat16)
        weighted = (
            product(weights[:, :rows], own_ref[:, HEAD:])
            + product(weights[:, rows : 2 * rows], last_ref[:, HEAD:])
            + product(weights[:, 2 * rows :], prior_values)
        )
        out_ref[step * count : (step + 1) * count] = (weighted / totals).astype(jnp.bfloat16)


def decode_kernel(len_ref, sums_ref, bias_ref, cache_ref, out_ref):
    request = pl.program_id(0)
    length = len_ref[request]
    slots, _, width = cache_ref.shape[1:]
    heads = width // HEAD

    def rounded(part, factor):
        total = (sums_ref[part * GROUP : (part + 1) * GROUP] + bias_ref[part]) * factor
        return total.astype(jnp.bfloat16).astype(jnp.float32)

    query = rounded(0, HEAD ** (-0.5))
    own_key, own_value = rounded(1, 1.0), rounded(2, 1.0)
    member = lax.broadcasted_iota(jnp.int32, (GROUP, width), 0)
    lane_head = lax.broadcasted_iota(jnp.int32, (GROUP, width), 1) // HEAD
    spread = jnp.concatenate([query] * heads, axis=1)
    spread = jnp.where(member == lane_head, spread, 0.0).astype(jnp.bfloat16)
    pairs = cache_ref[0].reshape(slots * 2, width)
    scores = product_t(spread, pairs)
    lane = lax.broadcasted_iota(jnp.int32, (1, slots * 2), 1)
    slot = lane >> 1
    near = (slot < SINKS) | (slot > length - WINDOW)
    allowed = (slot < length) & near & ((lane & 1) == 0)
    scores = jnp.where(allowed, scores, NEG)
    own_score = jnp.sum(query * own_key, axis=1, keepdims=True)
    highest = jnp.maximum(jnp.max(scores, axis=1, keepdims=True), own_score)
    expd = jnp.exp(scores - highest)
    own_expd = jnp.exp(own_score - highest)
    totals = jnp.sum(expd, axis=1, keepdims=True) + own_expd
    weights = pltpu.roll(expd, 1, 1).astype(jnp.bfloat16)
    every = product(weights, pairs)
    index = lax.broadcasted_iota(jnp.int32, (GROUP, HEAD), 0)
    weighted = own_expd.astype(jnp.bfloat16).astype(jnp.float32) * own_value
    for head in range(heads):
        lanes = every[:, head * HEAD : (head + 1) * HEAD]
        weighted += jnp.where(index == head, lanes, 0.0)
    out_ref[0] = weighted / totals


def decode(lengths, sums, bias, cache):
    requests, slots, _, width = cache.shape
    return pl.pallas_call(
        decode_kernel,
        out_shape=jax.ShapeDtypeStruct((requests, GROUP, HEAD), jnp.float32),
        grid=(requests,),
        in_specs=[
            pl.BlockSpec(memory_space=pltpu.SMEM),
            pl.BlockSpec((3 * GROUP, HEAD), lambda r: (r, 0)),
            pl.BlockSpec(bias.shape, lambda r: (0, 0, 0)),
            pl.BlockSpec((1, slots, 2, width), lambda r: (r, 0, 0, 0)),
        ],
        out_specs=pl.BlockSpec((1, GROUP, HEAD), lambda r: (r, 0, 0)),
        compiler_params=pltpu.CompilerParams(vmem_limit_bytes=2 * SMALL_VMEM),
        name="decode",
    )(lengths, sums, bias, cache)


def pack_kernel(prefill_ref, decode_ref, out_ref):
    rows = prefill_ref.shape[0]
    extra = decode_ref[...].reshape(decode_ref.shape[0] * GROUP, HEAD).astype(jnp.bfloat16)
    out_ref[:rows] = prefill_ref[...]
    out_ref[rows:] = extra


def out_kernel(*refs):
    part_refs, w_refs = refs[: 2 * YS], refs[2 * YS : 2 * YS + XS]
    out_ref, in_ref, attn_ref, w_ref = refs[2 * YS + XS :]
    heads = attn_ref.shape[1] // HEAD
    rows = attn_ref.shape[0]
    tok_rows = rows // GROUP
    core = lax.axis_index("c")
    for index, ref in enumerate(part_refs):
        source_y = lax.rem(lax.axis_index("y") + (0, 3, 1, 2)[index % YS], YS)
        source_c = core if index < YS else 1 - core
        in_ref[source_y * CS + source_c] = ref[...]
    extra = in_ref[:, rows:].astype(jnp.float32)
    requests = extra.shape[1] // GROUP
    place = lax.broadcasted_iota(jnp.int32, (1, tok_rows, 1), 1)
    for head in range(heads):
        values = in_ref[head, :rows].reshape(GROUP, tok_rows, HEAD).astype(jnp.float32)
        for request in range(requests):
            first = request * GROUP + head
            row = extra[:, first : first + 1]
            values = jnp.where(place == tok_rows - requests + request, row, values)
        values = values.astype(jnp.bfloat16).reshape(rows, HEAD)
        attn_ref[:, head * HEAD : (head + 1) * HEAD] = values
    for step, ref in zip((0, 3, 1, 2), w_refs):
        w_ref[turned_x(step)] = ref[...]
    weights = w_ref[...].reshape(XS * w_ref.shape[1], w_ref.shape[2])
    out_ref[...] = product_t(attn_ref[...], weights).astype(jnp.bfloat16)


def final_kernel(in_ref, hid_ref, bias_ref, out_ref, row_ref):
    piece = in_ref.shape[2] // XS
    for member in range(GROUP):
        total = in_ref[member * ZS].astype(jnp.float32)
        for source in range(1, ZS):
            total += in_ref[member * ZS + source].astype(jnp.float32)
        for block in range(XS):
            first = (block * GROUP + member) * piece
            row_ref[:, first : first + piece] = total[:, block * piece : (block + 1) * piece]
    result = hid_ref[...].astype(jnp.float32) + row_ref[...] + bias_ref[...]
    result = result.astype(jnp.bfloat16)
    for target in range(ZS):
        out_ref[target] = result


def on_device(
    hidden,
    ln_gain,
    ln_bias,
    w_qkv,
    qkv_bias,
    w_out,
    out_bias,
    dec_cache,
    prior_kv,
    dec_len,
    offsets,
):
    me_z = lax.axis_index("z")
    tok_rows, width = hidden.shape
    dec_dev = dec_cache.shape[0]
    pre_dev = tok_rows - dec_dev
    head_width = w_qkv.shape[2]
    heads = head_width // HEAD
    pcb = prior_kv.shape[0]
    rows = GROUP * tok_rows
    half = w_qkv.shape[0] // 2

    turned = w_qkv.transpose(1, 0, 2)
    kv_own, q_own = turned[1:], turned[:1]
    kv_left = lax.ppermute(kv_own, "x", shift(XS, 1))
    kv_right = lax.ppermute(kv_own, "x", shift(XS, -1))
    kv_left, kv_right, q_own = lax.optimization_barrier((kv_left, kv_right, q_own))
    kv_far_a = lax.ppermute(kv_left[:, :half], "x", shift(XS, 1))
    kv_far_b = lax.ppermute(kv_right[:, half:], "x", shift(XS, -1))
    q_left = lax.ppermute(q_own, "x", shift(XS, 1))
    q_right = lax.ppermute(q_own, "x", shift(XS, -1))
    q_far_a = lax.ppermute(q_left[:, :half], "x", shift(XS, 1))
    q_far_b = lax.ppermute(q_right[:, half:], "x", shift(XS, -1))

    pieces = in_vmem(
        norm_kernel,
        bf16(GROUP, XS, tok_rows + pcb, width // (XS * GROUP)),
        [],
        [hidden, ln_gain[None], ln_bias[None], prior_kv],
    )
    pieces = lax.all_to_all(pieces, ("y", "c"), 0, 0, tiled=True)
    prior = in_vmem(split_kernel, (bf16(GROUP, 2, pcb, HEAD),) * XS, [], [pieces])
    prior = (
        prior[0],
        lax.ppermute(prior[1], "x", shift(XS, 1)),
        lax.ppermute(prior[2], "x", shift(XS, -1)),
        lax.ppermute(prior[3], "x", shift(XS, 2)),
    )

    kv_send, kv_keep, kv_extra = project(
        tok_rows, dec_dev, pieces, (kv_own, kv_left, kv_right, kv_far_a, kv_far_b)
    )
    kv_parts = reduce_partial(kv_send, kv_keep)
    own_kv = in_vmem(finish_kv_kernel, bf16(rows, 2 * HEAD), [], [kv_parts, qkv_bias])
    last_kv = lax.ppermute(own_kv, "x", [(0, 1), (2, 3)])

    q_far_a, q_far_b, w_out = lax.optimization_barrier((q_far_a, q_far_b, w_out))
    q_send, q_keep, _ = project(
        tok_rows, dec_dev, pieces, (q_own, q_left, q_right, q_far_a, q_far_b), kv_extra
    )
    q_parts = reduce_partial(q_send, q_keep)
    w_own = w_out.T
    w_left = lax.ppermute(w_own, "x", shift(XS, 1))
    w_right = lax.ppermute(w_own, "x", shift(XS, -1))
    w_far = lax.ppermute(w_own, "x", shift(XS, 2))

    queries, sums = in_vmem(
        finish_q_kernel,
        (
            bf16(rows, HEAD),
            jax.ShapeDtypeStruct((3 * GROUP * dec_dev, HEAD), jnp.float32),
        ),
        [],
        [q_parts, qkv_bias],
    )
    tied_kv, queries = lax.optimization_barrier((own_kv, queries))
    mine = lax.all_to_all(tied_kv.reshape(GROUP, tok_rows, 2 * HEAD), ("y", "c"), 0, 0, tiled=True)
    new_kv = mine[:heads].reshape(heads, tok_rows, 2, HEAD)
    new_kv = new_kv.transpose(1, 2, 0, 3).reshape(tok_rows, 2, head_width)
    prefilled = in_vmem(
        functools.partial(attend_kernel, pre_dev),
        bf16(rows, HEAD),
        [offsets],
        [queries, own_kv, last_kv, *prior],
    )
    head_bias = jnp.pad(qkv_bias.reshape(3, heads, HEAD), ((0, 0), (0, GROUP - heads), (0, 0)))
    prefilled, sums = lax.optimization_barrier((prefilled, sums))
    decoded = decode(dec_len, sums, head_bias, dec_cache)
    payload = in_vmem(pack_kernel, bf16(rows + dec_dev * GROUP, HEAD), [], [prefilled, decoded])
    payload, new_kv, w_left, w_right, w_far = lax.optimization_barrier(
        (payload, new_kv, w_left, w_right, w_far)
    )
    gathered = [payload] + [lax.ppermute(payload, "y", shift(YS, s)) for s in (1, -1, 2)]
    gathered += [lax.ppermute(part, "c", [(0, 1), (1, 0)]) for part in gathered]
    piece = w_own.shape[0]
    shares = in_vmem(
        out_kernel,
        bf16(rows, XS * piece),
        [],
        [*gathered, w_own, w_left, w_right, w_far],
        [
            pltpu.VMEM((GROUP, *payload.shape), jnp.bfloat16),
            pltpu.VMEM((rows, head_width), jnp.bfloat16),
            pltpu.VMEM((XS, piece, head_width), jnp.bfloat16),
        ],
    )
    slab = tok_rows // ZS
    shares = shares.reshape(GROUP * ZS, slab, XS * piece)
    shares = lax.all_to_all(shares, ("y", "c", "z"), 0, 0, tiled=True)
    residual = lax.dynamic_slice(hidden, (me_z * slab, 0), (slab, width))
    result = in_vmem(
        final_kernel,
        bf16(ZS, slab, width),
        [],
        [shares, residual, out_bias[None]],
        [pltpu.VMEM((slab, width), jnp.float32)],
    )
    result = lax.all_to_all(result, "z", 0, 0, tiled=True).reshape(tok_rows, width)
    return (result, new_kv)


def solution(mesh):
    fine = Mesh(mesh.devices.reshape(XS, YS, CS, ZS), ("x", "y", "c", "z"))
    tok = ("x", "y", "c")
    in_specs = (
        P(tok, None),
        P(),
        P(),
        P(tok, None, "z"),
        P(None, "z"),
        P("z", tok),
        P(),
        P(tok, None, None, "z"),
        P(tok, None, None, "z"),
        P(tok),
        P(),
    )
    out_specs = (P(tok, None), P(tok, None, "z"))

    return jax.shard_map(
        on_device, mesh=fine, in_specs=in_specs, out_specs=out_specs, check_vma=False
    )
```

```python
import functools

import jax
import jax.numpy as jnp
from jax import lax
from jax.experimental import pallas as pl
from jax.experimental.pallas import tpu as pltpu
from jax.sharding import Mesh, PartitionSpec as P


HEAD = 128
WINDOW = 512
SINKS = 4
NEG = -1e30
FAR_AWAY = 1 << 20
SMALL_VMEM = 16 << 20
XS, YS, CS, ZS = 4, 4, 2, 8
GROUP = YS * CS


def shift(axis_size, step):
    return [(i, (i + step) % axis_size) for i in range(axis_size)]


def in_vmem(kernel, out_shape, scalars, arrays, scratch=(), loaded=()):
    vmem = pl.BlockSpec(memory_space=pltpu.VMEM)
    held = [
        pltpu.with_memory_space_constraint(a, pltpu.HBM if i in loaded else pltpu.VMEM)
        for i, a in enumerate(arrays)
    ]
    return pl.pallas_call(
        kernel,
        out_shape=out_shape,
        in_specs=[pl.BlockSpec(memory_space=pltpu.SMEM)] * len(scalars) + [vmem] * len(arrays),
        out_specs=jax.tree.map(lambda _: vmem, out_shape),
        scratch_shapes=list(scratch),
        compiler_params=pltpu.CompilerParams(vmem_limit_bytes=SMALL_VMEM),
    )(*scalars, *held)


def bf16(*shape):
    return jax.ShapeDtypeStruct(shape, jnp.bfloat16)


def product(left, right):
    return jnp.dot(left, right, preferred_element_type=jnp.float32)


def product_t(left, right):
    return lax.dot_general(
        left, right, (((1,), (1,)), ((), ())), preferred_element_type=jnp.float32
    )


def norm_kernel(hid_ref, gain_ref, bias_ref, prior_ref, out_ref):
    inputs = hid_ref[...].astype(jnp.float32)
    rows = inputs.shape[0]
    average = jnp.mean(inputs, axis=1, keepdims=True)
    centered = inputs - average
    spread = jnp.mean(centered * centered, axis=1, keepdims=True)
    normed = centered / jnp.sqrt(spread + 1e-05) * gain_ref[...] + bias_ref[...]
    piece = out_ref.shape[3]
    heads = prior_ref.shape[3] // HEAD
    for block in range(XS):
        earlier = prior_ref[:, block // 2, block % 2]
        for member in range(GROUP):
            first = (block * GROUP + member) * piece
            out_ref[member, block, :rows] = normed[:, first : first + piece].astype(jnp.bfloat16)
            head = min(member, heads - 1)
            out_ref[member, block, rows:, :HEAD] = earlier[:, head * HEAD : (head + 1) * HEAD]


def my_member():
    return lax.axis_index("y") * CS + lax.axis_index("c")


def turned_x(step):
    return lax.rem(lax.axis_index("x") + step, XS)


def split_kernel(in_ref, *out_refs):
    rows = in_ref.shape[2] - out_refs[0].shape[2]
    for step, out_ref in zip((0, 1, 3, 2), out_refs):
        request = turned_x(step) // 2
        out_ref[...] = in_ref[:, pl.ds(request * 2, 2), rows:, :HEAD]


def head_lanes(head, heads):
    return pl.ds(pl.multiple_of(jnp.minimum(head, heads - 1) * HEAD, HEAD), HEAD)


def project_kernel(with_extra, tok_rows, parts, *refs):
    in_ref, weight_refs = refs[0], refs[1:-3]
    send_ref, keep_ref, extra_ref = refs[-3:]
    if with_extra:
        weight_refs, more_ref = weight_refs[:-1], weight_refs[-1]
    core = lax.axis_index("c")
    members, piece = in_ref.shape[0], in_ref.shape[3]
    rows = members * tok_rows
    heads = weight_refs[0].shape[1] // HEAD
    together = 2 // parts
    width = parts * HEAD
    requests = extra_ref.shape[1] // (parts * GROUP)

    def rows_of(step):
        return in_ref[:, pl.ds(turned_x(step), 1), :tok_rows].reshape(rows, piece)

    inputs = [rows_of(step) for step in (0, 3, 1, 2)]

    def one_step(step, carry):
        for side, out_ref in ((1 - core, send_ref), (core, keep_ref)):
            slots = [together * step + index for index in range(together)]
            columns = [
                (part, head_lanes(CS * slot + side, heads))
                for slot in slots
                for part in range(parts)
            ]

            def wide(index):
                blocks = []
                for part, lanes in columns:
                    held = weight_refs[index * parts + part :]
                    held = held[:1] if index < XS - 1 or parts > 1 else held
                    blocks.append(jnp.concatenate([ref[:, lanes] for ref in held], axis=0))
                return jnp.concatenate(blocks, axis=1)

            total = product(inputs[0], wide(0))
            for index in range(1, XS):
                total += product(inputs[index], wide(index))
            for index, slot in enumerate(slots):
                mine = total[:, index * width : (index + 1) * width]
                out_ref[slot, :rows] = mine.astype(jnp.bfloat16)
                by_member = mine.reshape(members, tok_rows, width)
                for request in range(requests):
                    row = by_member[:, tok_rows - requests + request]
                    for part in range(parts):
                        place = (request * parts + part) * GROUP + CS * slot + side
                        lanes = slice(part * HEAD, (part + 1) * HEAD)
                        extra_ref[:, pl.ds(place, 1)] = row[:, None, lanes]
        return carry

    lax.fori_loop(0, YS // together, one_step, 0)
    if with_extra:
        for side, out_ref in ((1 - core, send_ref), (core, keep_ref)):
            for slot in range(YS):
                member = CS * slot + side
                for request in range(requests):
                    query = extra_ref[member, request * GROUP : (request + 1) * GROUP]
                    pair = more_ref[member, request * 2 * GROUP : (request + 1) * 2 * GROUP]
                    block = jnp.concatenate([query, pair], axis=0).astype(jnp.bfloat16)
                    if request == 0:
                        blocks = [block]
                    else:
                        blocks.append(block)
                out_ref[slot, rows:] = jnp.concatenate(blocks, axis=0)


def project(tok_rows, requests, parts, pieces, weights, more=None):
    rows = pieces.shape[0] * tok_rows
    extra = 0 if more is None else 3 * GROUP * requests
    out = bf16(YS, rows + extra, parts * HEAD)
    kept = jax.ShapeDtypeStruct((GROUP, parts * GROUP * requests, HEAD), jnp.float32)
    return in_vmem(
        functools.partial(project_kernel, more is not None, tok_rows, parts),
        (out, out, kept),
        [],
        [pieces, *weights] + ([] if more is None else [more]),
        loaded=range(1, 1 + len(weights)),
    )


def add_kernel(left_ref, right_ref, out_ref):
    total = left_ref[...].astype(jnp.float32) + right_ref[...].astype(jnp.float32)
    out_ref[...] = total.astype(jnp.bfloat16)


def reduce_partial(send, keep):
    swapped = lax.ppermute(send, "c", [(0, 1), (1, 0)])
    partial = in_vmem(add_kernel, bf16(*keep.shape), [], [keep, swapped])
    return lax.all_to_all(partial, "y", 0, 0, tiled=True)


def summed_rows(partial_ref):
    total = partial_ref[0].astype(jnp.float32)
    for source in range(1, YS):
        total += partial_ref[source].astype(jnp.float32)
    return total


def finish_kv_kernel(partial_ref, bias_ref, out_ref):
    lanes = head_lanes(my_member(), bias_ref.shape[1] // HEAD)
    bias = jnp.concatenate([bias_ref[1:2, lanes], bias_ref[2:3, lanes]], axis=1)
    out_ref[...] = (summed_rows(partial_ref) + bias).astype(jnp.bfloat16)


def finish_q_kernel(partial_ref, bias_ref, out_ref, decode_ref):
    lanes = head_lanes(my_member(), bias_ref.shape[1] // HEAD)
    total = summed_rows(partial_ref)
    rows = out_ref.shape[0]
    queries = (total[:rows] + bias_ref[0:1, lanes]) * HEAD ** (-0.5)
    out_ref[...] = queries.astype(jnp.bfloat16)
    decode_ref[...] = total[rows:]


def attend_kernel(pre_dev, offset_ref, query_ref, own_ref, last_ref, *refs):
    prior_refs, out_ref = refs[:-1], refs[-1]
    odd = lax.axis_index("x") % 2
    start = offset_ref[lax.axis_index("x") // 2]
    rows = query_ref.shape[0]
    count = rows // 4
    tok_rows = rows // GROUP
    half = pre_dev * GROUP

    def local(index):
        return (index // tok_rows) * pre_dev + index % tok_rows

    key_row = lax.broadcasted_iota(jnp.int32, (1, rows), 1)
    is_prefill = key_row % tok_rows < pre_dev
    own_pos = jnp.where(is_prefill, start + odd * half + local(key_row), FAR_AWAY)
    last_pos = jnp.where(is_prefill, start + local(key_row), FAR_AWAY)
    last_pos = jnp.where(odd == 1, last_pos, FAR_AWAY)
    old = prior_refs[0].shape[0] * prior_refs[0].shape[2]
    near_old = lax.broadcasted_iota(jnp.int32, (1, old), 1)
    old_pos = jnp.concatenate([turned_x(step) * old + near_old for step in (0, 3, 1, 2)], axis=1)
    old_pos = jnp.where(old_pos < start, old_pos, FAR_AWAY)
    key_pos = jnp.concatenate([own_pos, last_pos, old_pos], axis=1)
    prior_keys = jnp.concatenate([ref[:, 0].reshape(old, HEAD) for ref in prior_refs], axis=0)
    prior_values = jnp.concatenate([ref[:, 1].reshape(old, HEAD) for ref in prior_refs], axis=0)

    def one_step(step, carry):
        place = pl.ds(pl.multiple_of(step * count, count), count)
        queries = query_ref[place]
        row = step * count + lax.broadcasted_iota(jnp.int32, (count, 1), 0)
        query_pos = start + odd * half + local(row)
        scores = jnp.concatenate(
            [
                product_t(queries, own_ref[:, :HEAD]),
                product_t(queries, last_ref[:, :HEAD]),
                product_t(queries, prior_keys),
            ],
            axis=1,
        )
        near = (key_pos < SINKS) | (key_pos > query_pos - WINDOW)
        scores = jnp.where((key_pos <= query_pos) & near, scores, NEG)
        highest = jnp.max(scores, axis=1, keepdims=True)
        expd = jnp.exp(scores - highest)
        totals = jnp.sum(expd, axis=1, keepdims=True)
        weights = expd.astype(jnp.bfloat16)
        weighted = (
            product(weights[:, :rows], own_ref[:, HEAD:])
            + product(weights[:, rows : 2 * rows], last_ref[:, HEAD:])
            + product(weights[:, 2 * rows :], prior_values)
        )
        out_ref[place] = (weighted / totals).astype(jnp.bfloat16)
        return carry

    lax.fori_loop(0, rows // count, one_step, 0)


def decode_kernel(len_ref, sums_ref, bias_ref, cache_ref, out_ref):
    request = pl.program_id(0)
    length = len_ref[request]
    slots, _, width = cache_ref.shape[1:]
    heads = width // HEAD

    def rounded(part, factor):
        total = (sums_ref[part * GROUP : (part + 1) * GROUP] + bias_ref[part]) * factor
        return total.astype(jnp.bfloat16).astype(jnp.float32)

    query = rounded(0, HEAD ** (-0.5))
    own_key, own_value = rounded(1, 1.0), rounded(2, 1.0)
    member = lax.broadcasted_iota(jnp.int32, (GROUP, width), 0)
    lane_head = lax.broadcasted_iota(jnp.int32, (GROUP, width), 1) // HEAD
    spread = jnp.concatenate([query] * heads, axis=1)
    spread = jnp.where(member == lane_head, spread, 0.0).astype(jnp.bfloat16)
    pairs = cache_ref[0].reshape(slots * 2, width)
    scores = product_t(spread, pairs)
    lane = lax.broadcasted_iota(jnp.int32, (1, slots * 2), 1)
    slot = lane >> 1
    near = (slot < SINKS) | (slot > length - WINDOW)
    allowed = (slot < length) & near & ((lane & 1) == 0)
    scores = jnp.where(allowed, scores, NEG)
    own_score = jnp.sum(query * own_key, axis=1, keepdims=True)
    highest = jnp.maximum(jnp.max(scores, axis=1, keepdims=True), own_score)
    expd = jnp.exp(scores - highest)
    own_expd = jnp.exp(own_score - highest)
    totals = jnp.sum(expd, axis=1, keepdims=True) + own_expd
    weights = pltpu.roll(expd, 1, 1).astype(jnp.bfloat16)
    every = product(weights, pairs)
    index = lax.broadcasted_iota(jnp.int32, (GROUP, HEAD), 0)
    weighted = own_expd.astype(jnp.bfloat16).astype(jnp.float32) * own_value
    for head in range(heads):
        lanes = every[:, head * HEAD : (head + 1) * HEAD]
        weighted += jnp.where(index == head, lanes, 0.0)
    out_ref[0] = weighted / totals


def decode(lengths, sums, bias, cache):
    requests, slots, _, width = cache.shape
    return pl.pallas_call(
        decode_kernel,
        out_shape=jax.ShapeDtypeStruct((requests, GROUP, HEAD), jnp.float32),
        grid=(requests,),
        in_specs=[
            pl.BlockSpec(memory_space=pltpu.SMEM),
            pl.BlockSpec((3 * GROUP, HEAD), lambda r: (r, 0)),
            pl.BlockSpec(bias.shape, lambda r: (0, 0, 0)),
            pl.BlockSpec((1, slots, 2, width), lambda r: (r, 0, 0, 0)),
        ],
        out_specs=pl.BlockSpec((1, GROUP, HEAD), lambda r: (r, 0, 0)),
        compiler_params=pltpu.CompilerParams(vmem_limit_bytes=2 * SMALL_VMEM),
        name="decode",
    )(lengths, sums, bias, pltpu.with_memory_space_constraint(cache, pltpu.HBM))


def pack_kernel(prefill_ref, decode_ref, out_ref):
    rows = prefill_ref.shape[0]
    extra = decode_ref[...].reshape(decode_ref.shape[0] * GROUP, HEAD).astype(jnp.bfloat16)
    out_ref[:rows] = prefill_ref[...]
    out_ref[rows:] = extra


def out_kernel(*refs):
    part_refs, w_refs = refs[: 2 * YS], refs[2 * YS : 2 * YS + XS]
    out_ref, in_ref, attn_ref, w_ref = refs[2 * YS + XS :]
    heads = attn_ref.shape[1] // HEAD
    rows = attn_ref.shape[0]
    tok_rows = rows // GROUP
    core = lax.axis_index("c")
    for index, ref in enumerate(part_refs):
        source_y = lax.rem(lax.axis_index("y") + (0, 3, 1, 2)[index % YS], YS)
        source_c = core if index < YS else 1 - core
        in_ref[source_y * CS + source_c] = ref[...]
    extra = in_ref[:, rows:].astype(jnp.float32)
    requests = extra.shape[1] // GROUP
    place = lax.broadcasted_iota(jnp.int32, (1, tok_rows, 1), 1)
    for head in range(heads):
        values = in_ref[head, :rows].reshape(GROUP, tok_rows, HEAD).astype(jnp.float32)
        for request in range(requests):
            first = request * GROUP + head
            row = extra[:, first : first + 1]
            values = jnp.where(place == tok_rows - requests + request, row, values)
        values = values.astype(jnp.bfloat16).reshape(rows, HEAD)
        attn_ref[:, head * HEAD : (head + 1) * HEAD] = values
    for step, ref in zip((0, 3, 1, 2), w_refs):
        w_ref[turned_x(step)] = ref[...]
    weights = w_ref[...].reshape(XS * w_ref.shape[1], w_ref.shape[2])
    out_ref[...] = product_t(attn_ref[...], weights).astype(jnp.bfloat16)


def final_kernel(in_ref, hid_ref, bias_ref, out_ref, row_ref):
    piece = in_ref.shape[2] // XS
    for member in range(GROUP):
        total = in_ref[member * ZS].astype(jnp.float32)
        for source in range(1, ZS):
            total += in_ref[member * ZS + source].astype(jnp.float32)
        for block in range(XS):
            first = (block * GROUP + member) * piece
            row_ref[:, first : first + piece] = total[:, block * piece : (block + 1) * piece]
    result = hid_ref[...].astype(jnp.float32) + row_ref[...] + bias_ref[...]
    out_ref[...] = result.astype(jnp.bfloat16)


def place_kernel(*refs):
    part_refs, out_ref = refs[:-1], refs[-1]
    for step, ref in zip((0, 7, 1, 6, 2, 5, 3, 4), part_refs):
        out_ref[lax.rem(lax.axis_index("z") + step, ZS)] = ref[...]


def on_device(
    hidden,
    ln_gain,
    ln_bias,
    w_qkv,
    qkv_bias,
    w_out,
    out_bias,
    dec_cache,
    prior_kv,
    dec_len,
    offsets,
):
    me_z = lax.axis_index("z")
    tok_rows, width = hidden.shape
    dec_dev = dec_cache.shape[0]
    pre_dev = tok_rows - dec_dev
    head_width = w_qkv.shape[2]
    heads = head_width // HEAD
    pcb = prior_kv.shape[0]
    rows = GROUP * tok_rows
    half = w_qkv.shape[0] // 2

    def near(value):
        left = lax.ppermute(value, "x", shift(XS, 1))
        return left, lax.ppermute(value, "x", shift(XS, -1))

    turned = w_qkv.transpose(1, 0, 2)
    k_own, v_own = turned[1], turned[2]
    k_left, k_right = near(k_own)
    v_left, v_right = near(v_own)
    k_far = lax.ppermute(k_left, "x", shift(XS, 1))
    v_far = lax.ppermute(v_right, "x", shift(XS, -1))
    q_own = turned[0]
    v_left, v_right, q_own = lax.optimization_barrier((v_left, v_right, q_own))
    q_left, q_right = near(q_own)
    q_fars = (
        lax.ppermute(q_left[:half], "x", shift(XS, 1)),
        lax.ppermute(q_right[half:], "x", shift(XS, -1)),
    )
    kv_weights = (k_own, v_own, k_left, v_left, k_right, v_right, k_far, v_far)

    pieces = in_vmem(
        norm_kernel,
        bf16(GROUP, XS, tok_rows + pcb, width // (XS * GROUP)),
        [],
        [hidden, ln_gain[None], ln_bias[None], prior_kv],
    )
    pieces = lax.all_to_all(pieces, ("y", "c"), 0, 0, tiled=True)
    prior = in_vmem(split_kernel, (bf16(GROUP, 2, pcb, HEAD),) * XS, [], [pieces])
    prior = (
        prior[0],
        lax.ppermute(prior[1], "x", shift(XS, 1)),
        lax.ppermute(prior[2], "x", shift(XS, -1)),
        lax.ppermute(prior[3], "x", shift(XS, 2)),
    )

    kv_send, kv_keep, kv_extra = project(
        tok_rows, dec_dev, 2, pieces, kv_weights
    )
    kv_parts = reduce_partial(kv_send, kv_keep)
    own_kv = in_vmem(finish_kv_kernel, bf16(rows, 2 * HEAD), [], [kv_parts, qkv_bias])
    last_kv = lax.ppermute(own_kv, "x", [(0, 1), (2, 3)])

    q_weights = (q_own, q_left, q_right, *q_fars)
    q_send, q_keep, _ = project(
        tok_rows, dec_dev, 1, pieces, q_weights, kv_extra
    )
    q_parts = reduce_partial(q_send, q_keep)
    last_kv, w_out = lax.optimization_barrier((last_kv, w_out))
    w_own = w_out.T
    w_left = lax.ppermute(w_own, "x", shift(XS, 1))
    w_right = lax.ppermute(w_own, "x", shift(XS, -1))
    w_far = lax.ppermute(w_own, "x", shift(XS, 2))

    queries, sums = in_vmem(
        finish_q_kernel,
        (
            bf16(rows, HEAD),
            jax.ShapeDtypeStruct((3 * GROUP * dec_dev, HEAD), jnp.float32),
        ),
        [],
        [q_parts, qkv_bias],
    )
    tied_kv, queries = lax.optimization_barrier((own_kv, queries))
    mine = lax.all_to_all(tied_kv.reshape(GROUP, tok_rows, 2 * HEAD), ("y", "c"), 0, 0, tiled=True)
    new_kv = mine[:heads].reshape(heads, tok_rows, 2, HEAD)
    new_kv = new_kv.transpose(1, 2, 0, 3).reshape(tok_rows, 2, head_width)
    prefilled = in_vmem(
        functools.partial(attend_kernel, pre_dev),
        bf16(rows, HEAD),
        [offsets],
        [queries, own_kv, last_kv, *prior],
    )
    head_bias = jnp.pad(qkv_bias.reshape(3, heads, HEAD), ((0, 0), (0, GROUP - heads), (0, 0)))
    prefilled, sums = lax.optimization_barrier((prefilled, sums))
    decoded = decode(dec_len, sums, head_bias, dec_cache)
    payload = in_vmem(pack_kernel, bf16(rows + dec_dev * GROUP, HEAD), [], [prefilled, decoded])
    payload, new_kv, w_left, w_right, w_far = lax.optimization_barrier(
        (payload, new_kv, w_left, w_right, w_far)
    )
    gathered = [payload] + [lax.ppermute(payload, "y", shift(YS, s)) for s in (1, -1, 2)]
    gathered += [lax.ppermute(part, "c", [(0, 1), (1, 0)]) for part in gathered]
    piece = w_own.shape[0]
    shares = in_vmem(
        out_kernel,
        bf16(rows, XS * piece),
        [],
        [*gathered, w_own, w_left, w_right, w_far],
        [
            pltpu.VMEM((GROUP, *payload.shape), jnp.bfloat16),
            pltpu.VMEM((rows, head_width), jnp.bfloat16),
            pltpu.VMEM((XS, piece, head_width), jnp.bfloat16),
        ],
    )
    slab = tok_rows // ZS
    shares = shares.reshape(GROUP * ZS, slab, XS * piece)
    shares = lax.all_to_all(shares, ("y", "c", "z"), 0, 0, tiled=True)
    residual = lax.dynamic_slice(hidden, (me_z * slab, 0), (slab, width))
    result = in_vmem(
        final_kernel,
        bf16(slab, width),
        [],
        [shares, residual, out_bias[None]],
        [pltpu.VMEM((slab, width), jnp.float32)],
    )
    everyone = [result]
    up = down = result
    for step in range(ZS // 2):
        up = lax.ppermute(up, "z", shift(ZS, 1))
        everyone.append(up)
        if step < ZS // 2 - 1:
            down = lax.ppermute(down, "z", shift(ZS, -1))
            everyone.append(down)
    result = in_vmem(place_kernel, bf16(ZS, slab, width), [], everyone)
    result = result.reshape(tok_rows, width)
    return (result, new_kv)


def solution(mesh):
    fine = Mesh(mesh.devices.reshape(XS, YS, CS, ZS), ("x", "y", "c", "z"))
    tok = ("x", "y", "c")
    in_specs = (
        P(tok, None),
        P(),
        P(),
        P(tok, None, "z"),
        P(None, "z"),
        P("z", tok),
        P(),
        P(tok, None, None, "z"),
        P(tok, None, None, "z"),
        P(tok),
        P(),
    )
    out_specs = (P(tok, None), P(tok, None, "z"))

    return jax.shard_map(
        on_device, mesh=fine, in_specs=in_specs, out_specs=out_specs, check_vma=False
    )
```

```python
import functools

import jax
import jax.numpy as jnp
from jax import lax
from jax.experimental import pallas as pl
from jax.experimental.pallas import tpu as pltpu
from jax.sharding import Mesh, PartitionSpec as P


HEAD = 128
WINDOW = 512
SINKS = 4
NEG = -1e30
FAR_AWAY = 1 << 20
SMALL_VMEM = 16 << 20
XS, YS, CS, ZS = 4, 4, 2, 8
GROUP = YS * CS


def shift(axis_size, step):
    return [(i, (i + step) % axis_size) for i in range(axis_size)]


def in_vmem(kernel, out_shape, scalars, arrays, scratch=(), loaded=()):
    vmem = pl.BlockSpec(memory_space=pltpu.VMEM)
    held = [
        pltpu.with_memory_space_constraint(a, pltpu.HBM if i in loaded else pltpu.VMEM)
        for i, a in enumerate(arrays)
    ]
    return pl.pallas_call(
        kernel,
        out_shape=out_shape,
        in_specs=[pl.BlockSpec(memory_space=pltpu.SMEM)] * len(scalars) + [vmem] * len(arrays),
        out_specs=jax.tree.map(lambda _: vmem, out_shape),
        scratch_shapes=list(scratch),
        compiler_params=pltpu.CompilerParams(vmem_limit_bytes=SMALL_VMEM),
    )(*scalars, *held)


def bf16(*shape):
    return jax.ShapeDtypeStruct(shape, jnp.bfloat16)


def product(left, right):
    return jnp.dot(left, right, preferred_element_type=jnp.float32)


def product_t(left, right):
    return lax.dot_general(
        left, right, (((1,), (1,)), ((), ())), preferred_element_type=jnp.float32
    )


def norm_kernel(hid_ref, gain_ref, bias_ref, prior_ref, out_ref):
    inputs = hid_ref[...].astype(jnp.float32)
    rows = inputs.shape[0]
    average = jnp.mean(inputs, axis=1, keepdims=True)
    centered = inputs - average
    spread = jnp.mean(centered * centered, axis=1, keepdims=True)
    normed = centered / jnp.sqrt(spread + 1e-05) * gain_ref[...] + bias_ref[...]
    piece = out_ref.shape[3]
    heads = prior_ref.shape[3] // HEAD
    for block in range(XS):
        earlier = prior_ref[:, block // 2, block % 2]
        for member in range(GROUP):
            first = (block * GROUP + member) * piece
            out_ref[member, block, :rows] = normed[:, first : first + piece].astype(jnp.bfloat16)
            head = min(member, heads - 1)
            out_ref[member, block, rows:, :HEAD] = earlier[:, head * HEAD : (head + 1) * HEAD]


def my_member():
    return lax.axis_index("y") * CS + lax.axis_index("c")


def turned_x(step):
    return lax.rem(lax.axis_index("x") + step, XS)


def split_kernel(in_ref, *out_refs):
    rows = in_ref.shape[2] - out_refs[0].shape[2]
    for step, out_ref in zip((0, 1, 3, 2), out_refs):
        request = turned_x(step) // 2
        out_ref[...] = in_ref[:, pl.ds(request * 2, 2), rows:, :HEAD]


def head_lanes(head, heads):
    return pl.ds(pl.multiple_of(jnp.minimum(head, heads - 1) * HEAD, HEAD), HEAD)


def project_kernel(with_extra, tok_rows, parts, *refs):
    in_ref, weight_refs = refs[0], refs[1:-3]
    send_ref, keep_ref, extra_ref = refs[-3:]
    if with_extra:
        weight_refs, more_ref = weight_refs[:-1], weight_refs[-1]
    core = lax.axis_index("c")
    members, piece = in_ref.shape[0], in_ref.shape[3]
    rows = members * tok_rows
    heads = weight_refs[0].shape[1] // HEAD
    together = 2 // parts
    width = parts * HEAD
    requests = extra_ref.shape[1] // (parts * GROUP)

    def rows_of(step):
        return in_ref[:, pl.ds(turned_x(step), 1), :tok_rows].reshape(rows, piece)

    inputs = [rows_of(step) for step in (0, 3, 1, 2)]

    def one_step(step, carry):
        for side, out_ref in ((1 - core, send_ref), (core, keep_ref)):
            slots = [together * step + index for index in range(together)]
            columns = [
                (part, head_lanes(CS * slot + side, heads))
                for slot in slots
                for part in range(parts)
            ]

            def wide(index):
                blocks = []
                for part, lanes in columns:
                    held = weight_refs[index * parts + part :]
                    held = held[:1] if index < XS - 1 or parts > 1 else held
                    blocks.append(jnp.concatenate([ref[:, lanes] for ref in held], axis=0))
                return jnp.concatenate(blocks, axis=1)

            total = product(inputs[0], wide(0))
            for index in range(1, XS):
                total += product(inputs[index], wide(index))
            for index, slot in enumerate(slots):
                mine = total[:, index * width : (index + 1) * width]
                out_ref[slot, :rows] = mine.astype(jnp.bfloat16)
                by_member = mine.reshape(members, tok_rows, width)
                for request in range(requests):
                    row = by_member[:, tok_rows - requests + request]
                    for part in range(parts):
                        place = (request * parts + part) * GROUP + CS * slot + side
                        lanes = slice(part * HEAD, (part + 1) * HEAD)
                        extra_ref[:, pl.ds(place, 1)] = row[:, None, lanes]
        return carry

    lax.fori_loop(0, YS // together, one_step, 0)
    if with_extra:
        for side, out_ref in ((1 - core, send_ref), (core, keep_ref)):
            for slot in range(YS):
                member = CS * slot + side
                for request in range(requests):
                    query = extra_ref[member, request * GROUP : (request + 1) * GROUP]
                    pair = more_ref[member, request * 2 * GROUP : (request + 1) * 2 * GROUP]
                    block = jnp.concatenate([query, pair], axis=0).astype(jnp.bfloat16)
                    if request == 0:
                        blocks = [block]
                    else:
                        blocks.append(block)
                out_ref[slot, rows:] = jnp.concatenate(blocks, axis=0)


def project(tok_rows, requests, parts, pieces, weights, more=None):
    rows = pieces.shape[0] * tok_rows
    extra = 0 if more is None else 3 * GROUP * requests
    out = bf16(YS, rows + extra, parts * HEAD)
    kept = jax.ShapeDtypeStruct((GROUP, parts * GROUP * requests, HEAD), jnp.float32)
    return in_vmem(
        functools.partial(project_kernel, more is not None, tok_rows, parts),
        (out, out, kept),
        [],
        [pieces, *weights] + ([] if more is None else [more]),
        loaded=range(1, 1 + len(weights)),
    )


def add_kernel(left_ref, right_ref, out_ref):
    total = left_ref[...].astype(jnp.float32) + right_ref[...].astype(jnp.float32)
    out_ref[...] = total.astype(jnp.bfloat16)


def reduce_partial(send, keep):
    swapped = lax.ppermute(send, "c", [(0, 1), (1, 0)])
    partial = in_vmem(add_kernel, bf16(*keep.shape), [], [keep, swapped])
    return lax.all_to_all(partial, "y", 0, 0, tiled=True)


def summed_rows(partial_ref):
    total = partial_ref[0].astype(jnp.float32)
    for source in range(1, YS):
        total += partial_ref[source].astype(jnp.float32)
    return total


def finish_kv_kernel(partial_ref, bias_ref, out_ref):
    lanes = head_lanes(my_member(), bias_ref.shape[1] // HEAD)
    bias = jnp.concatenate([bias_ref[1:2, lanes], bias_ref[2:3, lanes]], axis=1)
    out_ref[...] = (summed_rows(partial_ref) + bias).astype(jnp.bfloat16)


def finish_q_kernel(partial_ref, bias_ref, out_ref, decode_ref):
    lanes = head_lanes(my_member(), bias_ref.shape[1] // HEAD)
    total = summed_rows(partial_ref)
    rows = out_ref.shape[0]
    queries = (total[:rows] + bias_ref[0:1, lanes]) * HEAD ** (-0.5)
    out_ref[...] = queries.astype(jnp.bfloat16)
    decode_ref[...] = total[rows:]


def attend_kernel(pre_dev, offset_ref, query_ref, own_ref, last_ref, *refs):
    prior_refs, out_ref = refs[:-1], refs[-1]
    odd = lax.axis_index("x") % 2
    start = offset_ref[lax.axis_index("x") // 2]
    rows = query_ref.shape[0]
    count = rows // 4
    tok_rows = rows // GROUP
    half = pre_dev * GROUP

    def local(index):
        return (index // tok_rows) * pre_dev + index % tok_rows

    key_row = lax.broadcasted_iota(jnp.int32, (1, rows), 1)
    is_prefill = key_row % tok_rows < pre_dev
    own_pos = jnp.where(is_prefill, start + odd * half + local(key_row), FAR_AWAY)
    last_pos = jnp.where(is_prefill, start + local(key_row), FAR_AWAY)
    last_pos = jnp.where(odd == 1, last_pos, FAR_AWAY)
    old = prior_refs[0].shape[0] * prior_refs[0].shape[2]
    near_old = lax.broadcasted_iota(jnp.int32, (1, old), 1)
    old_pos = jnp.concatenate([turned_x(step) * old + near_old for step in (0, 3, 1, 2)], axis=1)
    old_pos = jnp.where(old_pos < start, old_pos, FAR_AWAY)
    key_pos = jnp.concatenate([own_pos, last_pos, old_pos], axis=1)
    prior_keys = jnp.concatenate([ref[:, 0].reshape(old, HEAD) for ref in prior_refs], axis=0)
    prior_values = jnp.concatenate([ref[:, 1].reshape(old, HEAD) for ref in prior_refs], axis=0)

    def one_step(step, carry):
        place = pl.ds(pl.multiple_of(step * count, count), count)
        queries = query_ref[place]
        row = step * count + lax.broadcasted_iota(jnp.int32, (count, 1), 0)
        query_pos = start + odd * half + local(row)
        scores = jnp.concatenate(
            [
                product_t(queries, own_ref[:, :HEAD]),
                product_t(queries, last_ref[:, :HEAD]),
                product_t(queries, prior_keys),
            ],
            axis=1,
        )
        near = (key_pos < SINKS) | (key_pos > query_pos - WINDOW)
        scores = jnp.where((key_pos <= query_pos) & near, scores, NEG)
        highest = jnp.max(scores, axis=1, keepdims=True)
        expd = jnp.exp(scores - highest)
        totals = jnp.sum(expd, axis=1, keepdims=True)
        weights = expd.astype(jnp.bfloat16)
        weighted = (
            product(weights[:, :rows], own_ref[:, HEAD:])
            + product(weights[:, rows : 2 * rows], last_ref[:, HEAD:])
            + product(weights[:, 2 * rows :], prior_values)
        )
        out_ref[place] = (weighted / totals).astype(jnp.bfloat16)
        return carry

    lax.fori_loop(0, rows // count, one_step, 0)


def decode_kernel(len_ref, sums_ref, bias_ref, cache_ref, out_ref):
    request = pl.program_id(0)
    length = len_ref[request]
    slots, _, width = cache_ref.shape[1:]
    heads = width // HEAD

    def rounded(part, factor):
        total = (sums_ref[part * GROUP : (part + 1) * GROUP] + bias_ref[part]) * factor
        return total.astype(jnp.bfloat16).astype(jnp.float32)

    query = rounded(0, HEAD ** (-0.5))
    own_key, own_value = rounded(1, 1.0), rounded(2, 1.0)
    member = lax.broadcasted_iota(jnp.int32, (GROUP, width), 0)
    lane_head = lax.broadcasted_iota(jnp.int32, (GROUP, width), 1) // HEAD
    spread = jnp.concatenate([query] * heads, axis=1)
    spread = jnp.where(member == lane_head, spread, 0.0).astype(jnp.bfloat16)
    pairs = cache_ref[0].reshape(slots * 2, width)
    scores = product_t(spread, pairs)
    lane = lax.broadcasted_iota(jnp.int32, (1, slots * 2), 1)
    slot = lane >> 1
    near = (slot < SINKS) | (slot > length - WINDOW)
    allowed = (slot < length) & near & ((lane & 1) == 0)
    scores = jnp.where(allowed, scores, NEG)
    own_score = jnp.sum(query * own_key, axis=1, keepdims=True)
    highest = jnp.maximum(jnp.max(scores, axis=1, keepdims=True), own_score)
    expd = jnp.exp(scores - highest)
    own_expd = jnp.exp(own_score - highest)
    totals = jnp.sum(expd, axis=1, keepdims=True) + own_expd
    weights = pltpu.roll(expd, 1, 1).astype(jnp.bfloat16)
    every = product(weights, pairs)
    index = lax.broadcasted_iota(jnp.int32, (GROUP, HEAD), 0)
    weighted = own_expd.astype(jnp.bfloat16).astype(jnp.float32) * own_value
    for head in range(heads):
        lanes = every[:, head * HEAD : (head + 1) * HEAD]
        weighted += jnp.where(index == head, lanes, 0.0)
    out_ref[0] = weighted / totals


def decode(lengths, sums, bias, cache):
    requests, slots, _, width = cache.shape
    return pl.pallas_call(
        decode_kernel,
        out_shape=jax.ShapeDtypeStruct((requests, GROUP, HEAD), jnp.float32),
        grid=(requests,),
        in_specs=[
            pl.BlockSpec(memory_space=pltpu.SMEM),
            pl.BlockSpec((3 * GROUP, HEAD), lambda r: (r, 0)),
            pl.BlockSpec(bias.shape, lambda r: (0, 0, 0)),
            pl.BlockSpec((1, slots, 2, width), lambda r: (r, 0, 0, 0)),
        ],
        out_specs=pl.BlockSpec((1, GROUP, HEAD), lambda r: (r, 0, 0)),
        compiler_params=pltpu.CompilerParams(vmem_limit_bytes=2 * SMALL_VMEM),
        name="decode",
    )(lengths, sums, bias, pltpu.with_memory_space_constraint(cache, pltpu.HBM))


def pack_kernel(prefill_ref, decode_ref, out_ref):
    rows = prefill_ref.shape[0]
    extra = decode_ref[...].reshape(decode_ref.shape[0] * GROUP, HEAD).astype(jnp.bfloat16)
    out_ref[:rows] = prefill_ref[...]
    out_ref[rows:] = extra


def out_kernel(*refs):
    part_refs, w_refs = refs[: 2 * YS], refs[2 * YS : 2 * YS + XS]
    out_ref, in_ref, attn_ref, w_ref = refs[2 * YS + XS :]
    heads = attn_ref.shape[1] // HEAD
    rows = attn_ref.shape[0]
    tok_rows = rows // GROUP
    core = lax.axis_index("c")
    for index, ref in enumerate(part_refs):
        source_y = lax.rem(lax.axis_index("y") + (0, 3, 1, 2)[index % YS], YS)
        source_c = core if index < YS else 1 - core
        in_ref[source_y * CS + source_c] = ref[...]
    extra = in_ref[:, rows:].astype(jnp.float32)
    requests = extra.shape[1] // GROUP
    place = lax.broadcasted_iota(jnp.int32, (1, tok_rows, 1), 1)
    for head in range(heads):
        values = in_ref[head, :rows].reshape(GROUP, tok_rows, HEAD).astype(jnp.float32)
        for request in range(requests):
            first = request * GROUP + head
            row = extra[:, first : first + 1]
            values = jnp.where(place == tok_rows - requests + request, row, values)
        values = values.astype(jnp.bfloat16).reshape(rows, HEAD)
        attn_ref[:, head * HEAD : (head + 1) * HEAD] = values
    for step, ref in zip((0, 3, 1, 2), w_refs):
        w_ref[turned_x(step)] = ref[...]
    weights = w_ref[...].reshape(XS * w_ref.shape[1], w_ref.shape[2])
    out_ref[...] = product_t(attn_ref[...], weights).astype(jnp.bfloat16)


def final_kernel(in_ref, hid_ref, bias_ref, out_ref, row_ref):
    piece = in_ref.shape[2] // XS
    for member in range(GROUP):
        total = in_ref[member * ZS].astype(jnp.float32)
        for source in range(1, ZS):
            total += in_ref[member * ZS + source].astype(jnp.float32)
        for block in range(XS):
            first = (block * GROUP + member) * piece
            row_ref[:, first : first + piece] = total[:, block * piece : (block + 1) * piece]
    result = hid_ref[...].astype(jnp.float32) + row_ref[...] + bias_ref[...]
    out_ref[...] = result.astype(jnp.bfloat16)


def place_kernel(*refs):
    part_refs, out_ref = refs[:-1], refs[-1]
    for step, ref in zip((0, 7, 1, 6, 2, 5, 3, 4), part_refs):
        out_ref[lax.rem(lax.axis_index("z") + step, ZS)] = ref[...]


def on_device(
    hidden,
    ln_gain,
    ln_bias,
    w_qkv,
    qkv_bias,
    w_out,
    out_bias,
    dec_cache,
    prior_kv,
    dec_len,
    offsets,
):
    me_z = lax.axis_index("z")
    tok_rows, width = hidden.shape
    dec_dev = dec_cache.shape[0]
    pre_dev = tok_rows - dec_dev
    head_width = w_qkv.shape[2]
    heads = head_width // HEAD
    pcb = prior_kv.shape[0]
    rows = GROUP * tok_rows
    half = w_qkv.shape[0] // 2

    def near(value):
        left = lax.ppermute(value, "x", shift(XS, 1))
        return left, lax.ppermute(value, "x", shift(XS, -1))

    turned = w_qkv.transpose(1, 0, 2)
    k_own, turned = lax.optimization_barrier((turned[1], turned))
    v_own = turned[2]
    k_left, k_right = near(k_own)
    v_left, v_right = near(v_own)
    k_far = lax.ppermute(k_left, "x", shift(XS, 1))
    v_far = lax.ppermute(v_right, "x", shift(XS, -1))
    q_own = turned[0]
    v_left, v_right, q_own = lax.optimization_barrier((v_left, v_right, q_own))
    q_left, q_right = near(q_own)
    q_fars = (
        lax.ppermute(q_left[:half], "x", shift(XS, 1)),
        lax.ppermute(q_right[half:], "x", shift(XS, -1)),
    )
    kv_weights = (k_own, v_own, k_left, v_left, k_right, v_right, k_far, v_far)

    pieces = in_vmem(
        norm_kernel,
        bf16(GROUP, XS, tok_rows + pcb, width // (XS * GROUP)),
        [],
        [hidden, ln_gain[None], ln_bias[None], prior_kv],
    )
    pieces = lax.all_to_all(pieces, ("y", "c"), 0, 0, tiled=True)
    prior = in_vmem(split_kernel, (bf16(GROUP, 2, pcb, HEAD),) * XS, [], [pieces])
    prior = (
        prior[0],
        lax.ppermute(prior[1], "x", shift(XS, 1)),
        lax.ppermute(prior[2], "x", shift(XS, -1)),
        lax.ppermute(prior[3], "x", shift(XS, 2)),
    )

    kv_send, kv_keep, kv_extra = project(
        tok_rows, dec_dev, 2, pieces, kv_weights
    )
    kv_parts = reduce_partial(kv_send, kv_keep)
    own_kv = in_vmem(finish_kv_kernel, bf16(rows, 2 * HEAD), [], [kv_parts, qkv_bias])
    last_kv = lax.ppermute(own_kv, "x", [(0, 1), (2, 3)])

    q_weights = (q_own, q_left, q_right, *q_fars)
    q_send, q_keep, _ = project(
        tok_rows, dec_dev, 1, pieces, q_weights, kv_extra
    )
    q_parts = reduce_partial(q_send, q_keep)
    last_kv, w_out = lax.optimization_barrier((last_kv, w_out))
    w_own = w_out.T
    w_left = lax.ppermute(w_own, "x", shift(XS, 1))
    w_right = lax.ppermute(w_own, "x", shift(XS, -1))
    w_far = lax.ppermute(w_own, "x", shift(XS, 2))

    queries, sums = in_vmem(
        finish_q_kernel,
        (
            bf16(rows, HEAD),
            jax.ShapeDtypeStruct((3 * GROUP * dec_dev, HEAD), jnp.float32),
        ),
        [],
        [q_parts, qkv_bias],
    )
    tied_kv, queries = lax.optimization_barrier((own_kv, queries))
    mine = lax.all_to_all(tied_kv.reshape(GROUP, tok_rows, 2 * HEAD), ("y", "c"), 0, 0, tiled=True)
    prefilled = in_vmem(
        functools.partial(attend_kernel, pre_dev),
        bf16(rows, HEAD),
        [offsets],
        [queries, own_kv, last_kv, *prior],
    )
    head_bias = jnp.pad(qkv_bias.reshape(3, heads, HEAD), ((0, 0), (0, GROUP - heads), (0, 0)))
    prefilled, sums = lax.optimization_barrier((prefilled, sums))
    decoded = decode(dec_len, sums, head_bias, dec_cache)
    payload = in_vmem(pack_kernel, bf16(rows + dec_dev * GROUP, HEAD), [], [prefilled, decoded])
    payload, mine, w_left, w_right, w_far = lax.optimization_barrier(
        (payload, mine, w_left, w_right, w_far)
    )
    new_kv = mine[:heads].reshape(heads, tok_rows, 2, HEAD)
    new_kv = new_kv.transpose(1, 2, 0, 3).reshape(tok_rows, 2, head_width)
    gathered = [payload] + [lax.ppermute(payload, "y", shift(YS, s)) for s in (1, -1, 2)]
    gathered += [lax.ppermute(part, "c", [(0, 1), (1, 0)]) for part in gathered]
    piece = w_own.shape[0]
    shares = in_vmem(
        out_kernel,
        bf16(rows, XS * piece),
        [],
        [*gathered, w_own, w_left, w_right, w_far],
        [
            pltpu.VMEM((GROUP, *payload.shape), jnp.bfloat16),
            pltpu.VMEM((rows, head_width), jnp.bfloat16),
            pltpu.VMEM((XS, piece, head_width), jnp.bfloat16),
        ],
    )
    slab = tok_rows // ZS
    shares = shares.reshape(GROUP * ZS, slab, XS * piece)
    shares = lax.all_to_all(shares, ("y", "c", "z"), 0, 0, tiled=True)
    residual = lax.dynamic_slice(hidden, (me_z * slab, 0), (slab, width))
    result = in_vmem(
        final_kernel,
        bf16(slab, width),
        [],
        [shares, residual, out_bias[None]],
        [pltpu.VMEM((slab, width), jnp.float32)],
    )
    everyone = [result]
    up = down = result
    for step in range(ZS // 2):
        up = lax.ppermute(up, "z", shift(ZS, 1))
        everyone.append(up)
        if step < ZS // 2 - 1:
            down = lax.ppermute(down, "z", shift(ZS, -1))
            everyone.append(down)
    result = in_vmem(place_kernel, bf16(ZS, slab, width), [], everyone)
    result = result.reshape(tok_rows, width)
    return (result, new_kv)


def solution(mesh):
    fine = Mesh(mesh.devices.reshape(XS, YS, CS, ZS), ("x", "y", "c", "z"))
    tok = ("x", "y", "c")
    in_specs = (
        P(tok, None),
        P(),
        P(),
        P(tok, None, "z"),
        P(None, "z"),
        P("z", tok),
        P(),
        P(tok, None, None, "z"),
        P(tok, None, None, "z"),
        P(tok),
        P(),
    )
    out_specs = (P(tok, None), P(tok, None, "z"))

    return jax.shard_map(
        on_device, mesh=fine, in_specs=in_specs, out_specs=out_specs, check_vma=False
    )
```

```python
import functools

import jax
import jax.numpy as jnp
from jax import lax
from jax.experimental import pallas as pl
from jax.experimental.pallas import tpu as pltpu
from jax.sharding import Mesh, PartitionSpec as P


HEAD = 128
WINDOW = 512
SINKS = 4
NEG = -1e30
FAR_AWAY = 1 << 20
SMALL_VMEM = 16 << 20
XS, YS, CS, ZS = 4, 4, 2, 8
GROUP = YS * CS


def shift(axis_size, step):
    return [(i, (i + step) % axis_size) for i in range(axis_size)]


def in_vmem(kernel, out_shape, scalars, arrays, scratch=(), loaded=()):
    vmem = pl.BlockSpec(memory_space=pltpu.VMEM)
    held = [
        pltpu.with_memory_space_constraint(a, pltpu.HBM if i in loaded else pltpu.VMEM)
        for i, a in enumerate(arrays)
    ]
    return pl.pallas_call(
        kernel,
        out_shape=out_shape,
        in_specs=[pl.BlockSpec(memory_space=pltpu.SMEM)] * len(scalars) + [vmem] * len(arrays),
        out_specs=jax.tree.map(lambda _: vmem, out_shape),
        scratch_shapes=list(scratch),
        compiler_params=pltpu.CompilerParams(vmem_limit_bytes=SMALL_VMEM),
    )(*scalars, *held)


def bf16(*shape):
    return jax.ShapeDtypeStruct(shape, jnp.bfloat16)


def product(left, right):
    return jnp.dot(left, right, preferred_element_type=jnp.float32)


def product_t(left, right):
    return lax.dot_general(
        left, right, (((1,), (1,)), ((), ())), preferred_element_type=jnp.float32
    )


def norm_kernel(hid_ref, gain_ref, bias_ref, prior_ref, out_ref):
    inputs = hid_ref[...].astype(jnp.float32)
    rows = inputs.shape[0]
    average = jnp.mean(inputs, axis=1, keepdims=True)
    centered = inputs - average
    spread = jnp.mean(centered * centered, axis=1, keepdims=True)
    normed = centered / jnp.sqrt(spread + 1e-05) * gain_ref[...] + bias_ref[...]
    piece = out_ref.shape[3]
    heads = prior_ref.shape[3] // HEAD
    for block in range(XS):
        earlier = prior_ref[:, block // 2, block % 2]
        for member in range(GROUP):
            first = (block * GROUP + member) * piece
            out_ref[member, block, :rows] = normed[:, first : first + piece].astype(jnp.bfloat16)
            head = min(member, heads - 1)
            out_ref[member, block, rows:, :HEAD] = earlier[:, head * HEAD : (head + 1) * HEAD]


def my_member():
    return lax.axis_index("y") * CS + lax.axis_index("c")


def turned_x(step):
    return lax.rem(lax.axis_index("x") + step, XS)


def split_kernel(in_ref, *out_refs):
    rows = in_ref.shape[2] - out_refs[0].shape[2]
    for step, out_ref in zip((0, 1, 3, 2), out_refs):
        request = turned_x(step) // 2
        out_ref[...] = in_ref[:, pl.ds(request * 2, 2), rows:, :HEAD]


def head_lanes(head, heads):
    return pl.ds(pl.multiple_of(jnp.minimum(head, heads - 1) * HEAD, HEAD), HEAD)


def project_kernel(with_extra, tok_rows, parts, *refs):
    in_ref, weight_refs = refs[0], refs[1:-3]
    send_ref, keep_ref, extra_ref = refs[-3:]
    if with_extra:
        weight_refs, more_ref = weight_refs[:-1], weight_refs[-1]
    core = lax.axis_index("c")
    members, piece = in_ref.shape[0], in_ref.shape[3]
    rows = members * tok_rows
    heads = weight_refs[0].shape[1] // HEAD
    together = 2 // parts
    width = parts * HEAD
    segments = len(weight_refs) // (XS * parts)
    requests = extra_ref.shape[1] // (parts * GROUP)

    def rows_of(step):
        return in_ref[:, pl.ds(turned_x(step), 1), :tok_rows].reshape(rows, piece)

    inputs = [rows_of(step) for step in (0, 3, 1, 2)]

    def one_step(step, carry):
        for side, out_ref in ((1 - core, send_ref), (core, keep_ref)):
            slots = [together * step + index for index in range(together)]
            columns = [
                (part, head_lanes(CS * slot + side, heads))
                for slot in slots
                for part in range(parts)
            ]

            def wide(index):
                blocks = []
                for part, lanes in columns:
                    first_ref = (index * parts + part) * segments
                    held = weight_refs[first_ref : first_ref + segments]
                    blocks.append(jnp.concatenate([ref[:, lanes] for ref in held], axis=0))
                return jnp.concatenate(blocks, axis=1)

            total = product(inputs[0], wide(0))
            for index in range(1, XS):
                total += product(inputs[index], wide(index))
            for index, slot in enumerate(slots):
                mine = total[:, index * width : (index + 1) * width]
                out_ref[slot, :rows] = mine.astype(jnp.bfloat16)
                by_member = mine.reshape(members, tok_rows, width)
                for request in range(requests):
                    row = by_member[:, tok_rows - requests + request]
                    for part in range(parts):
                        place = (request * parts + part) * GROUP + CS * slot + side
                        lanes = slice(part * HEAD, (part + 1) * HEAD)
                        extra_ref[:, pl.ds(place, 1)] = row[:, None, lanes]
        return carry

    lax.fori_loop(0, YS // together, one_step, 0)
    if with_extra:
        for side, out_ref in ((1 - core, send_ref), (core, keep_ref)):
            for slot in range(YS):
                member = CS * slot + side
                for request in range(requests):
                    query = extra_ref[member, request * GROUP : (request + 1) * GROUP]
                    pair = more_ref[member, request * 2 * GROUP : (request + 1) * 2 * GROUP]
                    block = jnp.concatenate([query, pair], axis=0).astype(jnp.bfloat16)
                    if request == 0:
                        blocks = [block]
                    else:
                        blocks.append(block)
                out_ref[slot, rows:] = jnp.concatenate(blocks, axis=0)


def project(tok_rows, requests, parts, pieces, weights, more=None):
    rows = pieces.shape[0] * tok_rows
    extra = 0 if more is None else 3 * GROUP * requests
    out = bf16(YS, rows + extra, parts * HEAD)
    kept = jax.ShapeDtypeStruct((GROUP, parts * GROUP * requests, HEAD), jnp.float32)
    return in_vmem(
        functools.partial(project_kernel, more is not None, tok_rows, parts),
        (out, out, kept),
        [],
        [pieces, *weights] + ([] if more is None else [more]),
        loaded=range(1, 1 + len(weights)),
    )


def add_kernel(left_ref, right_ref, out_ref):
    total = left_ref[...].astype(jnp.float32) + right_ref[...].astype(jnp.float32)
    out_ref[...] = total.astype(jnp.bfloat16)


def reduce_partial(send, keep):
    swapped = lax.ppermute(send, "c", [(0, 1), (1, 0)])
    partial = in_vmem(add_kernel, bf16(*keep.shape), [], [keep, swapped])
    return lax.all_to_all(partial, "y", 0, 0, tiled=True)


def summed_rows(partial_ref):
    total = partial_ref[0].astype(jnp.float32)
    for source in range(1, YS):
        total += partial_ref[source].astype(jnp.float32)
    return total


def finish_kv_kernel(partial_ref, bias_ref, out_ref):
    lanes = head_lanes(my_member(), bias_ref.shape[1] // HEAD)
    bias = jnp.concatenate([bias_ref[1:2, lanes], bias_ref[2:3, lanes]], axis=1)
    out_ref[...] = (summed_rows(partial_ref) + bias).astype(jnp.bfloat16)


def finish_q_kernel(partial_ref, bias_ref, out_ref, decode_ref):
    lanes = head_lanes(my_member(), bias_ref.shape[1] // HEAD)
    total = summed_rows(partial_ref)
    rows = out_ref.shape[0]
    queries = (total[:rows] + bias_ref[0:1, lanes]) * HEAD ** (-0.5)
    out_ref[...] = queries.astype(jnp.bfloat16)
    decode_ref[...] = total[rows:]


def attend_kernel(pre_dev, offset_ref, query_ref, own_ref, last_ref, *refs):
    prior_refs, out_ref = refs[:-1], refs[-1]
    odd = lax.axis_index("x") % 2
    start = offset_ref[lax.axis_index("x") // 2]
    rows = query_ref.shape[0]
    count = rows // 4
    tok_rows = rows // GROUP
    half = pre_dev * GROUP

    def local(index):
        return (index // tok_rows) * pre_dev + index % tok_rows

    key_row = lax.broadcasted_iota(jnp.int32, (1, rows), 1)
    is_prefill = key_row % tok_rows < pre_dev
    own_pos = jnp.where(is_prefill, start + odd * half + local(key_row), FAR_AWAY)
    last_pos = jnp.where(is_prefill, start + local(key_row), FAR_AWAY)
    last_pos = jnp.where(odd == 1, last_pos, FAR_AWAY)
    old = prior_refs[0].shape[0] * prior_refs[0].shape[2]
    near_old = lax.broadcasted_iota(jnp.int32, (1, old), 1)
    old_pos = jnp.concatenate([turned_x(step) * old + near_old for step in (0, 3, 1, 2)], axis=1)
    old_pos = jnp.where(old_pos < start, old_pos, FAR_AWAY)
    key_pos = jnp.concatenate([own_pos, last_pos, old_pos], axis=1)
    prior_keys = jnp.concatenate([ref[:, 0].reshape(old, HEAD) for ref in prior_refs], axis=0)
    prior_values = jnp.concatenate([ref[:, 1].reshape(old, HEAD) for ref in prior_refs], axis=0)

    def one_step(step, carry):
        place = pl.ds(pl.multiple_of(step * count, count), count)
        queries = query_ref[place]
        row = step * count + lax.broadcasted_iota(jnp.int32, (count, 1), 0)
        query_pos = start + odd * half + local(row)
        scores = jnp.concatenate(
            [
                product_t(queries, own_ref[:, :HEAD]),
                product_t(queries, last_ref[:, :HEAD]),
                product_t(queries, prior_keys),
            ],
            axis=1,
        )
        near = (key_pos < SINKS) | (key_pos > query_pos - WINDOW)
        scores = jnp.where((key_pos <= query_pos) & near, scores, NEG)
        highest = jnp.max(scores, axis=1, keepdims=True)
        expd = jnp.exp(scores - highest)
        totals = jnp.sum(expd, axis=1, keepdims=True)
        weights = expd.astype(jnp.bfloat16)
        weighted = (
            product(weights[:, :rows], own_ref[:, HEAD:])
            + product(weights[:, rows : 2 * rows], last_ref[:, HEAD:])
            + product(weights[:, 2 * rows :], prior_values)
        )
        out_ref[place] = (weighted / totals).astype(jnp.bfloat16)
        return carry

    lax.fori_loop(0, rows // count, one_step, 0)


def decode_kernel(len_ref, sums_ref, bias_ref, cache_ref, out_ref):
    request = pl.program_id(0)
    length = len_ref[request]
    slots, _, width = cache_ref.shape[1:]
    heads = width // HEAD

    def rounded(part, factor):
        total = (sums_ref[part * GROUP : (part + 1) * GROUP] + bias_ref[part]) * factor
        return total.astype(jnp.bfloat16).astype(jnp.float32)

    query = rounded(0, HEAD ** (-0.5))
    own_key, own_value = rounded(1, 1.0), rounded(2, 1.0)
    member = lax.broadcasted_iota(jnp.int32, (GROUP, width), 0)
    lane_head = lax.broadcasted_iota(jnp.int32, (GROUP, width), 1) // HEAD
    spread = jnp.concatenate([query] * heads, axis=1)
    spread = jnp.where(member == lane_head, spread, 0.0).astype(jnp.bfloat16)
    pairs = cache_ref[0].reshape(slots * 2, width)
    scores = product_t(spread, pairs)
    lane = lax.broadcasted_iota(jnp.int32, (1, slots * 2), 1)
    slot = lane >> 1
    near = (slot < SINKS) | (slot > length - WINDOW)
    allowed = (slot < length) & near & ((lane & 1) == 0)
    scores = jnp.where(allowed, scores, NEG)
    own_score = jnp.sum(query * own_key, axis=1, keepdims=True)
    highest = jnp.maximum(jnp.max(scores, axis=1, keepdims=True), own_score)
    expd = jnp.exp(scores - highest)
    own_expd = jnp.exp(own_score - highest)
    totals = jnp.sum(expd, axis=1, keepdims=True) + own_expd
    weights = pltpu.roll(expd, 1, 1).astype(jnp.bfloat16)
    every = product(weights, pairs)
    index = lax.broadcasted_iota(jnp.int32, (GROUP, HEAD), 0)
    weighted = own_expd.astype(jnp.bfloat16).astype(jnp.float32) * own_value
    for head in range(heads):
        lanes = every[:, head * HEAD : (head + 1) * HEAD]
        weighted += jnp.where(index == head, lanes, 0.0)
    out_ref[0] = weighted / totals


def decode(lengths, sums, bias, cache):
    requests, slots, _, width = cache.shape
    return pl.pallas_call(
        decode_kernel,
        out_shape=jax.ShapeDtypeStruct((requests, GROUP, HEAD), jnp.float32),
        grid=(requests,),
        in_specs=[
            pl.BlockSpec(memory_space=pltpu.SMEM),
            pl.BlockSpec((3 * GROUP, HEAD), lambda r: (r, 0)),
            pl.BlockSpec(bias.shape, lambda r: (0, 0, 0)),
            pl.BlockSpec((1, slots, 2, width), lambda r: (r, 0, 0, 0)),
        ],
        out_specs=pl.BlockSpec((1, GROUP, HEAD), lambda r: (r, 0, 0)),
        compiler_params=pltpu.CompilerParams(vmem_limit_bytes=2 * SMALL_VMEM),
        name="decode",
    )(lengths, sums, bias, pltpu.with_memory_space_constraint(cache, pltpu.HBM))


def pack_kernel(prefill_ref, decode_ref, out_ref):
    rows = prefill_ref.shape[0]
    extra = decode_ref[...].reshape(decode_ref.shape[0] * GROUP, HEAD).astype(jnp.bfloat16)
    out_ref[:rows] = prefill_ref[...]
    out_ref[rows:] = extra


def out_kernel(*refs):
    part_refs, w_refs = refs[: 2 * YS], refs[2 * YS : 2 * YS + XS]
    out_ref, in_ref, attn_ref, w_ref = refs[2 * YS + XS :]
    heads = attn_ref.shape[1] // HEAD
    rows = attn_ref.shape[0]
    tok_rows = rows // GROUP
    core = lax.axis_index("c")
    for index, ref in enumerate(part_refs):
        source_y = lax.rem(lax.axis_index("y") + (0, 3, 1, 2)[index % YS], YS)
        source_c = core if index < YS else 1 - core
        in_ref[source_y * CS + source_c] = ref[...]
    extra = in_ref[:, rows:].astype(jnp.float32)
    requests = extra.shape[1] // GROUP
    place = lax.broadcasted_iota(jnp.int32, (1, tok_rows, 1), 1)
    for head in range(heads):
        values = in_ref[head, :rows].reshape(GROUP, tok_rows, HEAD).astype(jnp.float32)
        for request in range(requests):
            first = request * GROUP + head
            row = extra[:, first : first + 1]
            values = jnp.where(place == tok_rows - requests + request, row, values)
        values = values.astype(jnp.bfloat16).reshape(rows, HEAD)
        attn_ref[:, head * HEAD : (head + 1) * HEAD] = values
    for step, ref in zip((0, 3, 1, 2), w_refs):
        w_ref[turned_x(step)] = ref[...]
    weights = w_ref[...].reshape(XS * w_ref.shape[1], w_ref.shape[2])
    out_ref[...] = product_t(attn_ref[...], weights).astype(jnp.bfloat16)


def final_kernel(in_ref, hid_ref, bias_ref, out_ref, row_ref):
    piece = in_ref.shape[2] // XS
    for member in range(GROUP):
        total = in_ref[member * ZS].astype(jnp.float32)
        for source in range(1, ZS):
            total += in_ref[member * ZS + source].astype(jnp.float32)
        for block in range(XS):
            first = (block * GROUP + member) * piece
            row_ref[:, first : first + piece] = total[:, block * piece : (block + 1) * piece]
    result = hid_ref[...].astype(jnp.float32) + row_ref[...] + bias_ref[...]
    out_ref[...] = result.astype(jnp.bfloat16)


def place_kernel(*refs):
    part_refs, out_ref = refs[:-1], refs[-1]
    for step, ref in zip((0, 7, 1, 6, 2, 5, 3, 4), part_refs):
        out_ref[lax.rem(lax.axis_index("z") + step, ZS)] = ref[...]


def on_device(
    hidden,
    ln_gain,
    ln_bias,
    w_qkv,
    qkv_bias,
    w_out,
    out_bias,
    dec_cache,
    prior_kv,
    dec_len,
    offsets,
):
    me_z = lax.axis_index("z")
    tok_rows, width = hidden.shape
    dec_dev = dec_cache.shape[0]
    pre_dev = tok_rows - dec_dev
    head_width = w_qkv.shape[2]
    heads = head_width // HEAD
    pcb = prior_kv.shape[0]
    rows = GROUP * tok_rows
    half = w_qkv.shape[0] // 2

    def near(value):
        left = lax.ppermute(value, "x", shift(XS, 1))
        return left, lax.ppermute(value, "x", shift(XS, -1))

    turned = w_qkv.transpose(1, 0, 2)
    k_own, turned = lax.optimization_barrier((turned[1], turned))
    v_own = turned[2]
    k_left, k_right = near(k_own)
    v_left, v_right = near(v_own)
    k_far = lax.ppermute(k_left, "x", shift(XS, 1))
    v_far = lax.ppermute(v_right, "x", shift(XS, -1))
    q_halves = (turned[0, :half], turned[0, half:])
    v_left, v_right, q_halves = lax.optimization_barrier((v_left, v_right, q_halves))
    q_lefts, q_rights = zip(*[near(part) for part in q_halves])
    q_fars = (
        lax.ppermute(q_lefts[0], "x", shift(XS, 1)),
        lax.ppermute(q_rights[1], "x", shift(XS, -1)),
    )
    kv_weights = (k_own, v_own, k_left, v_left, k_right, v_right, k_far, v_far)

    pieces = in_vmem(
        norm_kernel,
        bf16(GROUP, XS, tok_rows + pcb, width // (XS * GROUP)),
        [],
        [hidden, ln_gain[None], ln_bias[None], prior_kv],
    )
    pieces = lax.all_to_all(pieces, ("y", "c"), 0, 0, tiled=True)
    prior = in_vmem(split_kernel, (bf16(GROUP, 2, pcb, HEAD),) * XS, [], [pieces])
    prior = (
        prior[0],
        lax.ppermute(prior[1], "x", shift(XS, 1)),
        lax.ppermute(prior[2], "x", shift(XS, -1)),
        lax.ppermute(prior[3], "x", shift(XS, 2)),
    )

    kv_send, kv_keep, kv_extra = project(
        tok_rows, dec_dev, 2, pieces, kv_weights
    )
    kv_parts = reduce_partial(kv_send, kv_keep)
    own_kv = in_vmem(finish_kv_kernel, bf16(rows, 2 * HEAD), [], [kv_parts, qkv_bias])
    last_kv = lax.ppermute(own_kv, "x", [(0, 1), (2, 3)])

    q_weights = (*q_halves, *q_lefts, *q_rights, *q_fars)
    q_send, q_keep, _ = project(
        tok_rows, dec_dev, 1, pieces, q_weights, kv_extra
    )
    q_parts = reduce_partial(q_send, q_keep)
    q_fars, w_out = lax.optimization_barrier((q_fars, w_out))
    w_own = w_out.T
    w_left = lax.ppermute(w_own, "x", shift(XS, 1))
    w_right = lax.ppermute(w_own, "x", shift(XS, -1))
    w_far = lax.ppermute(w_own, "x", shift(XS, 2))

    queries, sums = in_vmem(
        finish_q_kernel,
        (
            bf16(rows, HEAD),
            jax.ShapeDtypeStruct((3 * GROUP * dec_dev, HEAD), jnp.float32),
        ),
        [],
        [q_parts, qkv_bias],
    )
    tied_kv, queries = lax.optimization_barrier((own_kv, queries))
    mine = lax.all_to_all(tied_kv.reshape(GROUP, tok_rows, 2 * HEAD), ("y", "c"), 0, 0, tiled=True)
    prefilled = in_vmem(
        functools.partial(attend_kernel, pre_dev),
        bf16(rows, HEAD),
        [offsets],
        [queries, own_kv, last_kv, *prior],
    )
    head_bias = jnp.pad(qkv_bias.reshape(3, heads, HEAD), ((0, 0), (0, GROUP - heads), (0, 0)))
    prefilled, sums = lax.optimization_barrier((prefilled, sums))
    decoded = decode(dec_len, sums, head_bias, dec_cache)
    payload = in_vmem(pack_kernel, bf16(rows + dec_dev * GROUP, HEAD), [], [prefilled, decoded])
    payload, w_left, w_right, w_far = lax.optimization_barrier((payload, w_left, w_right, w_far))
    gathered = [payload] + [lax.ppermute(payload, "y", shift(YS, s)) for s in (1, -1, 2)]
    gathered += [lax.ppermute(part, "c", [(0, 1), (1, 0)]) for part in gathered]
    piece = w_own.shape[0]
    shares = in_vmem(
        out_kernel,
        bf16(rows, XS * piece),
        [],
        [*gathered, w_own, w_left, w_right, w_far],
        [
            pltpu.VMEM((GROUP, *payload.shape), jnp.bfloat16),
            pltpu.VMEM((rows, head_width), jnp.bfloat16),
            pltpu.VMEM((XS, piece, head_width), jnp.bfloat16),
        ],
    )
    shares, mine = lax.optimization_barrier((shares, mine))
    new_kv = mine[:heads].reshape(heads, tok_rows, 2, HEAD)
    new_kv = new_kv.transpose(1, 2, 0, 3).reshape(tok_rows, 2, head_width)
    slab = tok_rows // ZS
    shares = shares.reshape(GROUP * ZS, slab, XS * piece)
    shares = lax.all_to_all(shares, ("y", "c", "z"), 0, 0, tiled=True)
    residual = lax.dynamic_slice(hidden, (me_z * slab, 0), (slab, width))
    result = in_vmem(
        final_kernel,
        bf16(slab, width),
        [],
        [shares, residual, out_bias[None]],
        [pltpu.VMEM((slab, width), jnp.float32)],
    )
    everyone = [result]
    up = down = result
    for step in range(ZS // 2):
        up = lax.ppermute(up, "z", shift(ZS, 1))
        everyone.append(up)
        if step < ZS // 2 - 1:
            down = lax.ppermute(down, "z", shift(ZS, -1))
            everyone.append(down)
    result = in_vmem(place_kernel, bf16(ZS, slab, width), [], everyone)
    result = result.reshape(tok_rows, width)
    return (result, new_kv)


def solution(mesh):
    fine = Mesh(mesh.devices.reshape(XS, YS, CS, ZS), ("x", "y", "c", "z"))
    tok = ("x", "y", "c")
    in_specs = (
        P(tok, None),
        P(),
        P(),
        P(tok, None, "z"),
        P(None, "z"),
        P("z", tok),
        P(),
        P(tok, None, None, "z"),
        P(tok, None, None, "z"),
        P(tok),
        P(),
    )
    out_specs = (P(tok, None), P(tok, None, "z"))

    return jax.shard_map(
        on_device, mesh=fine, in_specs=in_specs, out_specs=out_specs, check_vma=False
    )
```

```python
import functools

import jax
import jax.numpy as jnp
from jax import lax
from jax.experimental import pallas as pl
from jax.experimental.pallas import tpu as pltpu
from jax.sharding import Mesh, PartitionSpec as P


HEAD = 128
WINDOW = 512
SINKS = 4
NEG = -1e30
FAR_AWAY = 1 << 20
SMALL_VMEM = 16 << 20
XS, YS, CS, ZS = 4, 4, 2, 8
GROUP = YS * CS


def shift(axis_size, step):
    return [(i, (i + step) % axis_size) for i in range(axis_size)]


def in_vmem(kernel, out_shape, scalars, arrays, scratch=(), loaded=()):
    vmem = pl.BlockSpec(memory_space=pltpu.VMEM)
    held = [
        pltpu.with_memory_space_constraint(a, pltpu.HBM if i in loaded else pltpu.VMEM)
        for i, a in enumerate(arrays)
    ]
    return pl.pallas_call(
        kernel,
        out_shape=out_shape,
        in_specs=[pl.BlockSpec(memory_space=pltpu.SMEM)] * len(scalars) + [vmem] * len(arrays),
        out_specs=jax.tree.map(lambda _: vmem, out_shape),
        scratch_shapes=list(scratch),
        compiler_params=pltpu.CompilerParams(vmem_limit_bytes=SMALL_VMEM),
    )(*scalars, *held)


def bf16(*shape):
    return jax.ShapeDtypeStruct(shape, jnp.bfloat16)


def product(left, right):
    return jnp.dot(left, right, preferred_element_type=jnp.float32)


def product_t(left, right):
    return lax.dot_general(
        left, right, (((1,), (1,)), ((), ())), preferred_element_type=jnp.float32
    )


def norm_kernel(hid_ref, gain_ref, bias_ref, prior_ref, out_ref):
    inputs = hid_ref[...].astype(jnp.float32)
    rows = inputs.shape[0]
    average = jnp.mean(inputs, axis=1, keepdims=True)
    centered = inputs - average
    spread = jnp.mean(centered * centered, axis=1, keepdims=True)
    normed = centered / jnp.sqrt(spread + 1e-05) * gain_ref[...] + bias_ref[...]
    piece = out_ref.shape[3]
    heads = prior_ref.shape[3] // HEAD
    for block in range(XS):
        earlier = prior_ref[:, block // 2, block % 2]
        for member in range(GROUP):
            first = (block * GROUP + member) * piece
            out_ref[member, block, :rows] = normed[:, first : first + piece].astype(jnp.bfloat16)
            head = min(member, heads - 1)
            out_ref[member, block, rows:, :HEAD] = earlier[:, head * HEAD : (head + 1) * HEAD]


def my_member():
    return lax.axis_index("y") * CS + lax.axis_index("c")


def turned_x(step):
    return lax.rem(lax.axis_index("x") + step, XS)


def split_kernel(in_ref, *out_refs):
    rows = in_ref.shape[2] - out_refs[0].shape[2]
    for step, out_ref in zip((0, 1, 3, 2), out_refs):
        request = turned_x(step) // 2
        out_ref[...] = in_ref[:, pl.ds(request * 2, 2), rows:, :HEAD]


def head_lanes(head, heads):
    return pl.ds(pl.multiple_of(jnp.minimum(head, heads - 1) * HEAD, HEAD), HEAD)


def project_kernel(with_extra, tok_rows, parts, *refs):
    in_ref, weight_refs = refs[0], refs[1:-3]
    send_ref, keep_ref, extra_ref = refs[-3:]
    if with_extra:
        weight_refs, more_ref = weight_refs[:-1], weight_refs[-1]
    core = lax.axis_index("c")
    members, piece = in_ref.shape[0], in_ref.shape[3]
    rows = members * tok_rows
    heads = weight_refs[0].shape[1] // HEAD
    together = 2 // parts
    width = parts * HEAD
    segments = len(weight_refs) // (XS * parts)
    requests = extra_ref.shape[1] // (parts * GROUP)

    def rows_of(step):
        return in_ref[:, pl.ds(turned_x(step), 1), :tok_rows].reshape(rows, piece)

    inputs = [rows_of(step) for step in (0, 3, 1, 2)]

    def one_step(step, carry):
        for side, out_ref in ((1 - core, send_ref), (core, keep_ref)):
            slots = [together * step + index for index in range(together)]
            columns = [
                (part, head_lanes(CS * slot + side, heads))
                for slot in slots
                for part in range(parts)
            ]

            def wide(index):
                blocks = []
                for part, lanes in columns:
                    first_ref = (index * parts + part) * segments
                    held = weight_refs[first_ref : first_ref + segments]
                    blocks.append(jnp.concatenate([ref[:, lanes] for ref in held], axis=0))
                return jnp.concatenate(blocks, axis=1)

            total = product(inputs[0], wide(0))
            for index in range(1, XS):
                total += product(inputs[index], wide(index))
            for index, slot in enumerate(slots):
                mine = total[:, index * width : (index + 1) * width]
                out_ref[slot, :rows] = mine.astype(jnp.bfloat16)
                by_member = mine.reshape(members, tok_rows, width)
                for request in range(requests):
                    row = by_member[:, tok_rows - requests + request]
                    for part in range(parts):
                        place = (request * parts + part) * GROUP + CS * slot + side
                        lanes = slice(part * HEAD, (part + 1) * HEAD)
                        extra_ref[:, pl.ds(place, 1)] = row[:, None, lanes]
        return carry

    lax.fori_loop(0, YS // together, one_step, 0)
    if with_extra:
        for side, out_ref in ((1 - core, send_ref), (core, keep_ref)):
            for slot in range(YS):
                member = CS * slot + side
                for request in range(requests):
                    query = extra_ref[member, request * GROUP : (request + 1) * GROUP]
                    pair = more_ref[member, request * 2 * GROUP : (request + 1) * 2 * GROUP]
                    block = jnp.concatenate([query, pair], axis=0).astype(jnp.bfloat16)
                    if request == 0:
                        blocks = [block]
                    else:
                        blocks.append(block)
                out_ref[slot, rows:] = jnp.concatenate(blocks, axis=0)


def project(tok_rows, requests, parts, pieces, weights, more=None):
    rows = pieces.shape[0] * tok_rows
    extra = 0 if more is None else 3 * GROUP * requests
    out = bf16(YS, rows + extra, parts * HEAD)
    kept = jax.ShapeDtypeStruct((GROUP, parts * GROUP * requests, HEAD), jnp.float32)
    return in_vmem(
        functools.partial(project_kernel, more is not None, tok_rows, parts),
        (out, out, kept),
        [],
        [pieces, *weights] + ([] if more is None else [more]),
        loaded=range(1, 1 + len(weights)),
    )


def add_kernel(left_ref, right_ref, out_ref):
    total = left_ref[...].astype(jnp.float32) + right_ref[...].astype(jnp.float32)
    out_ref[...] = total.astype(jnp.bfloat16)


def reduce_partial(send, keep):
    swapped = lax.ppermute(send, "c", [(0, 1), (1, 0)])
    partial = in_vmem(add_kernel, bf16(*keep.shape), [], [keep, swapped])
    return lax.all_to_all(partial, "y", 0, 0, tiled=True)


def summed_rows(partial_ref):
    total = partial_ref[0].astype(jnp.float32)
    for source in range(1, YS):
        total += partial_ref[source].astype(jnp.float32)
    return total


def finish_kv_kernel(partial_ref, bias_ref, out_ref):
    lanes = head_lanes(my_member(), bias_ref.shape[1] // HEAD)
    bias = jnp.concatenate([bias_ref[1:2, lanes], bias_ref[2:3, lanes]], axis=1)
    out_ref[...] = (summed_rows(partial_ref) + bias).astype(jnp.bfloat16)


def finish_q_kernel(partial_ref, bias_ref, out_ref, decode_ref):
    lanes = head_lanes(my_member(), bias_ref.shape[1] // HEAD)
    total = summed_rows(partial_ref)
    rows = out_ref.shape[0]
    queries = (total[:rows] + bias_ref[0:1, lanes]) * HEAD ** (-0.5)
    out_ref[...] = queries.astype(jnp.bfloat16)
    decode_ref[...] = total[rows:]


def attend_kernel(pre_dev, offset_ref, query_ref, own_ref, last_ref, *refs):
    prior_refs, out_ref = refs[:-1], refs[-1]
    odd = lax.axis_index("x") % 2
    start = offset_ref[lax.axis_index("x") // 2]
    rows = query_ref.shape[0]
    count = rows // 4
    tok_rows = rows // GROUP
    half = pre_dev * GROUP

    def local(index):
        return (index // tok_rows) * pre_dev + index % tok_rows

    key_row = lax.broadcasted_iota(jnp.int32, (1, rows), 1)
    is_prefill = key_row % tok_rows < pre_dev
    own_pos = jnp.where(is_prefill, start + odd * half + local(key_row), FAR_AWAY)
    last_pos = jnp.where(is_prefill, start + local(key_row), FAR_AWAY)
    last_pos = jnp.where(odd == 1, last_pos, FAR_AWAY)
    old = prior_refs[0].shape[0] * prior_refs[0].shape[2]
    near_old = lax.broadcasted_iota(jnp.int32, (1, old), 1)
    old_pos = jnp.concatenate([turned_x(step) * old + near_old for step in (0, 3, 1, 2)], axis=1)
    old_pos = jnp.where(old_pos < start, old_pos, FAR_AWAY)
    key_pos = jnp.concatenate([own_pos, last_pos, old_pos], axis=1)
    prior_keys = jnp.concatenate([ref[:, 0].reshape(old, HEAD) for ref in prior_refs], axis=0)
    prior_values = jnp.concatenate([ref[:, 1].reshape(old, HEAD) for ref in prior_refs], axis=0)

    def one_step(step, carry):
        place = pl.ds(pl.multiple_of(step * count, count), count)
        queries = query_ref[place]
        row = step * count + lax.broadcasted_iota(jnp.int32, (count, 1), 0)
        query_pos = start + odd * half + local(row)
        scores = jnp.concatenate(
            [
                product_t(queries, own_ref[:, :HEAD]),
                product_t(queries, last_ref[:, :HEAD]),
                product_t(queries, prior_keys),
            ],
            axis=1,
        )
        near = (key_pos < SINKS) | (key_pos > query_pos - WINDOW)
        scores = jnp.where((key_pos <= query_pos) & near, scores, NEG)
        highest = jnp.max(scores, axis=1, keepdims=True)
        expd = jnp.exp(scores - highest)
        totals = jnp.sum(expd, axis=1, keepdims=True)
        weights = expd.astype(jnp.bfloat16)
        weighted = (
            product(weights[:, :rows], own_ref[:, HEAD:])
            + product(weights[:, rows : 2 * rows], last_ref[:, HEAD:])
            + product(weights[:, 2 * rows :], prior_values)
        )
        out_ref[place] = (weighted / totals).astype(jnp.bfloat16)
        return carry

    lax.fori_loop(0, rows // count, one_step, 0)


def decode_kernel(len_ref, sums_ref, bias_ref, cache_ref, out_ref):
    request = pl.program_id(0)
    length = len_ref[request]
    slots, _, width = cache_ref.shape[1:]
    heads = width // HEAD

    def rounded(part, factor):
        total = (sums_ref[part * GROUP : (part + 1) * GROUP] + bias_ref[part]) * factor
        return total.astype(jnp.bfloat16).astype(jnp.float32)

    query = rounded(0, HEAD ** (-0.5))
    own_key, own_value = rounded(1, 1.0), rounded(2, 1.0)
    member = lax.broadcasted_iota(jnp.int32, (GROUP, width), 0)
    lane_head = lax.broadcasted_iota(jnp.int32, (GROUP, width), 1) // HEAD
    spread = jnp.concatenate([query] * heads, axis=1)
    spread = jnp.where(member == lane_head, spread, 0.0).astype(jnp.bfloat16)
    pairs = cache_ref[0].reshape(slots * 2, width)
    scores = product_t(spread, pairs)
    lane = lax.broadcasted_iota(jnp.int32, (1, slots * 2), 1)
    slot = lane >> 1
    near = (slot < SINKS) | (slot > length - WINDOW)
    allowed = (slot < length) & near & ((lane & 1) == 0)
    scores = jnp.where(allowed, scores, NEG)
    own_score = jnp.sum(query * own_key, axis=1, keepdims=True)
    highest = jnp.maximum(jnp.max(scores, axis=1, keepdims=True), own_score)
    expd = jnp.exp(scores - highest)
    own_expd = jnp.exp(own_score - highest)
    totals = jnp.sum(expd, axis=1, keepdims=True) + own_expd
    weights = pltpu.roll(expd, 1, 1).astype(jnp.bfloat16)
    every = product(weights, pairs)
    index = lax.broadcasted_iota(jnp.int32, (GROUP, HEAD), 0)
    weighted = own_expd.astype(jnp.bfloat16).astype(jnp.float32) * own_value
    for head in range(heads):
        lanes = every[:, head * HEAD : (head + 1) * HEAD]
        weighted += jnp.where(index == head, lanes, 0.0)
    out_ref[0] = weighted / totals


def decode(lengths, sums, bias, cache):
    requests, slots, _, width = cache.shape
    return pl.pallas_call(
        decode_kernel,
        out_shape=jax.ShapeDtypeStruct((requests, GROUP, HEAD), jnp.float32),
        grid=(requests,),
        in_specs=[
            pl.BlockSpec(memory_space=pltpu.SMEM),
            pl.BlockSpec((3 * GROUP, HEAD), lambda r: (r, 0)),
            pl.BlockSpec(bias.shape, lambda r: (0, 0, 0)),
            pl.BlockSpec((1, slots, 2, width), lambda r: (r, 0, 0, 0)),
        ],
        out_specs=pl.BlockSpec((1, GROUP, HEAD), lambda r: (r, 0, 0)),
        compiler_params=pltpu.CompilerParams(vmem_limit_bytes=2 * SMALL_VMEM),
        name="decode",
    )(lengths, sums, bias, pltpu.with_memory_space_constraint(cache, pltpu.HBM))


def pack_kernel(prefill_ref, decode_ref, out_ref):
    rows = prefill_ref.shape[0]
    extra = decode_ref[...].reshape(decode_ref.shape[0] * GROUP, HEAD).astype(jnp.bfloat16)
    out_ref[:rows] = prefill_ref[...]
    out_ref[rows:] = extra


def out_kernel(*refs):
    part_refs, w_refs = refs[: 2 * YS], refs[2 * YS : 2 * YS + XS]
    out_ref, in_ref, attn_ref, w_ref = refs[2 * YS + XS :]
    heads = attn_ref.shape[1] // HEAD
    rows = attn_ref.shape[0]
    tok_rows = rows // GROUP
    core = lax.axis_index("c")
    for index, ref in enumerate(part_refs):
        source_y = lax.rem(lax.axis_index("y") + (0, 3, 1, 2)[index % YS], YS)
        source_c = core if index < YS else 1 - core
        in_ref[source_y * CS + source_c] = ref[...]
    extra = in_ref[:, rows:].astype(jnp.float32)
    requests = extra.shape[1] // GROUP
    place = lax.broadcasted_iota(jnp.int32, (1, tok_rows, 1), 1)
    for head in range(heads):
        values = in_ref[head, :rows].reshape(GROUP, tok_rows, HEAD).astype(jnp.float32)
        for request in range(requests):
            first = request * GROUP + head
            row = extra[:, first : first + 1]
            values = jnp.where(place == tok_rows - requests + request, row, values)
        values = values.astype(jnp.bfloat16).reshape(rows, HEAD)
        attn_ref[:, head * HEAD : (head + 1) * HEAD] = values
    for step, ref in zip((0, 3, 1, 2), w_refs):
        w_ref[turned_x(step)] = ref[...]
    weights = w_ref[...].reshape(XS * w_ref.shape[1], w_ref.shape[2])
    out_ref[...] = product_t(attn_ref[...], weights).astype(jnp.bfloat16)


def final_kernel(in_ref, hid_ref, bias_ref, out_ref, row_ref):
    piece = in_ref.shape[2] // XS
    for member in range(GROUP):
        total = in_ref[member * ZS].astype(jnp.float32)
        for source in range(1, ZS):
            total += in_ref[member * ZS + source].astype(jnp.float32)
        for block in range(XS):
            first = (block * GROUP + member) * piece
            row_ref[:, first : first + piece] = total[:, block * piece : (block + 1) * piece]
    result = hid_ref[...].astype(jnp.float32) + row_ref[...] + bias_ref[...]
    out_ref[...] = result.astype(jnp.bfloat16)


def place_kernel(*refs):
    part_refs, out_ref = refs[:-1], refs[-1]
    for step, ref in zip((0, 7, 1, 6, 2, 5, 3, 4), part_refs):
        out_ref[lax.rem(lax.axis_index("z") + step, ZS)] = ref[...]


def on_device(
    hidden,
    ln_gain,
    ln_bias,
    w_qkv,
    qkv_bias,
    w_out,
    out_bias,
    dec_cache,
    prior_kv,
    dec_len,
    offsets,
):
    me_z = lax.axis_index("z")
    tok_rows, width = hidden.shape
    dec_dev = dec_cache.shape[0]
    pre_dev = tok_rows - dec_dev
    head_width = w_qkv.shape[2]
    heads = head_width // HEAD
    pcb = prior_kv.shape[0]
    rows = GROUP * tok_rows
    half = w_qkv.shape[0] // 2

    def near(value):
        left = lax.ppermute(value, "x", shift(XS, 1))
        return left, lax.ppermute(value, "x", shift(XS, -1))

    turned = w_qkv.transpose(1, 0, 2)
    k_own, turned = lax.optimization_barrier((turned[1], turned))
    v_own = turned[2]
    k_left, k_right = near(k_own)
    v_left, v_right = near(v_own)
    k_far = lax.ppermute(k_left, "x", shift(XS, 1))
    v_far = lax.ppermute(v_right, "x", shift(XS, -1))
    q_halves = (turned[0, :half], turned[0, half:])
    v_left, v_right, q_halves = lax.optimization_barrier((v_left, v_right, q_halves))
    q_lefts, q_rights = zip(*[near(part) for part in q_halves])
    q_fars = (
        lax.ppermute(q_lefts[0], "x", shift(XS, 1)),
        lax.ppermute(q_rights[1], "x", shift(XS, -1)),
    )
    kv_weights = (k_own, v_own, k_left, v_left, k_right, v_right, k_far, v_far)

    pieces = in_vmem(
        norm_kernel,
        bf16(GROUP, XS, tok_rows + pcb, width // (XS * GROUP)),
        [],
        [hidden, ln_gain[None], ln_bias[None], prior_kv],
    )
    pieces = lax.all_to_all(pieces, ("y", "c"), 0, 0, tiled=True)
    prior = in_vmem(split_kernel, (bf16(GROUP, 2, pcb, HEAD),) * XS, [], [pieces])
    prior = (
        prior[0],
        lax.ppermute(prior[1], "x", shift(XS, 1)),
        lax.ppermute(prior[2], "x", shift(XS, -1)),
        lax.ppermute(prior[3], "x", shift(XS, 2)),
    )

    kv_send, kv_keep, kv_extra = project(
        tok_rows, dec_dev, 2, pieces, kv_weights
    )
    kv_parts = reduce_partial(kv_send, kv_keep)
    own_kv = in_vmem(finish_kv_kernel, bf16(rows, 2 * HEAD), [], [kv_parts, qkv_bias])
    last_kv = lax.ppermute(own_kv, "x", [(0, 1), (2, 3)])

    q_weights = (*q_halves, *q_lefts, *q_rights, *q_fars)
    q_send, q_keep, _ = project(
        tok_rows, dec_dev, 1, pieces, q_weights, kv_extra
    )
    q_parts = reduce_partial(q_send, q_keep)
    q_fars, w_out = lax.optimization_barrier((q_fars, w_out))
    w_own = w_out.T
    w_left = lax.ppermute(w_own, "x", shift(XS, 1))
    w_right = lax.ppermute(w_own, "x", shift(XS, -1))
    w_far = lax.ppermute(w_own, "x", shift(XS, 2))

    queries, sums = in_vmem(
        finish_q_kernel,
        (
            bf16(rows, HEAD),
            jax.ShapeDtypeStruct((3 * GROUP * dec_dev, HEAD), jnp.float32),
        ),
        [],
        [q_parts, qkv_bias],
    )
    prefilled = in_vmem(
        functools.partial(attend_kernel, pre_dev),
        bf16(rows, HEAD),
        [offsets],
        [queries, own_kv, last_kv, *prior],
        loaded=range(3, 3 + XS),
    )
    head_bias = jnp.pad(qkv_bias.reshape(3, heads, HEAD), ((0, 0), (0, GROUP - heads), (0, 0)))
    prefilled, sums = lax.optimization_barrier((prefilled, sums))
    decoded = decode(dec_len, sums, head_bias, dec_cache)
    payload = in_vmem(pack_kernel, bf16(rows + dec_dev * GROUP, HEAD), [], [prefilled, decoded])
    gathered = [payload] + [lax.ppermute(payload, "y", shift(YS, s)) for s in (1, -1, 2)]
    gathered += [lax.ppermute(part, "c", [(0, 1), (1, 0)]) for part in gathered]
    piece = w_own.shape[0]
    shares = in_vmem(
        out_kernel,
        bf16(rows, XS * piece),
        [],
        [*gathered, w_own, w_left, w_right, w_far],
        [
            pltpu.VMEM((GROUP, *payload.shape), jnp.bfloat16),
            pltpu.VMEM((rows, head_width), jnp.bfloat16),
            pltpu.VMEM((XS, piece, head_width), jnp.bfloat16),
        ],
    )
    slab = tok_rows // ZS
    shares = shares.reshape(GROUP * ZS, slab, XS * piece)
    shares = lax.all_to_all(shares, ("y", "c", "z"), 0, 0, tiled=True)
    residual = lax.dynamic_slice(hidden, (me_z * slab, 0), (slab, width))
    result = in_vmem(
        final_kernel,
        bf16(slab, width),
        [],
        [shares, residual, out_bias[None]],
        [pltpu.VMEM((slab, width), jnp.float32)],
    )
    tied_kv, result = lax.optimization_barrier((own_kv, result))
    mine = lax.all_to_all(tied_kv.reshape(GROUP, tok_rows, 2 * HEAD), ("y", "c"), 0, 0, tiled=True)
    new_kv = mine[:heads].reshape(heads, tok_rows, 2, HEAD)
    new_kv = new_kv.transpose(1, 2, 0, 3).reshape(tok_rows, 2, head_width)
    everyone = [result]
    up = down = result
    for step in range(ZS // 2):
        up = lax.ppermute(up, "z", shift(ZS, 1))
        everyone.append(up)
        if step < ZS // 2 - 1:
            down = lax.ppermute(down, "z", shift(ZS, -1))
            everyone.append(down)
    result = in_vmem(place_kernel, bf16(ZS, slab, width), [], everyone)
    result = result.reshape(tok_rows, width)
    return (result, new_kv)


def solution(mesh):
    fine = Mesh(mesh.devices.reshape(XS, YS, CS, ZS), ("x", "y", "c", "z"))
    tok = ("x", "y", "c")
    in_specs = (
        P(tok, None),
        P(),
        P(),
        P(tok, None, "z"),
        P(None, "z"),
        P("z", tok),
        P(),
        P(tok, None, None, "z"),
        P(tok, None, None, "z"),
        P(tok),
        P(),
    )
    out_specs = (P(tok, None), P(tok, None, "z"))

    return jax.shard_map(
        on_device, mesh=fine, in_specs=in_specs, out_specs=out_specs, check_vma=False
    )
```
